32 devices in a mesh: ulysses: 2 (over y), blk: 16 (over z, x, core).
Axes of the slice: x: 2, y: 2, z: 4, core: 2. Of those that a mesh axis runs over, the one named last changes fastest.
Arguments:
- query_first: bfloat16 [32, 64, 2, 128], P('blk', None, 'ulysses'), may hold values from -6 to 6
- query_second: bfloat16 [32, 64, 2, 128], P('blk', None, 'ulysses'), may hold values from -6 to 6
- key_first: bfloat16 [32, 64, 2, 128], P('blk', None, 'ulysses'), may hold values from -6 to 6
- key_second: bfloat16 [32, 64, 2, 128], P('blk', None, 'ulysses'), may hold values from -6 to 6
- values: bfloat16 [32, 64, 2, 256], P('blk', None, 'ulysses'), may hold values from -6 to 6
- out_first: bfloat16 [32, 64, 2, 256], P('blk', None, 'ulysses'), may hold values from -6 to 6, as said below
- out_second: bfloat16 [32, 64, 2, 256], P('blk', None, 'ulysses'), may hold values from -6 to 6, as said below
- log_totals: float32 [2, 2, 32, 64], P('ulysses', None, 'blk'), as said below
- lambdas: float32 [2], P('ulysses'), may hold values from 0.1 to 0.8
- norm_gain: float32 [2, 256], P('ulysses'), may hold values from 0.1 to 1.9
- cotangent: bfloat16 [32, 64, 2, 256], P('blk', 'ulysses'), may hold values from -6 to 6
- block_of: int32 [32], replicated, may hold values from 0 to 31, as said below
Outputs:
- grad_query_first: bfloat16 [32, 64, 2, 128], P('blk', None, 'ulysses')
- grad_query_second: bfloat16 [32, 64, 2, 128], P('blk', None, 'ulysses')
- grad_key_first: bfloat16 [32, 64, 2, 128], P('blk', None, 'ulysses')
- grad_key_second: bfloat16 [32, 64, 2, 128], P('blk', None, 'ulysses')
- grad_values: bfloat16 [32, 64, 2, 256], P('blk', None, 'ulysses')
The draws below stay inside these ranges and needn't reach their ends.
Inputs may be any that keep to these rules, and one draw needn't show every extreme that they name: `block_of`: slots 2d and 2d + 1 hold blocks c_d and 31 - c_d, where c_0 to c_last form a permutation of 0 to 15. `out_first`: the causal softmax average of values under the first pair's scaled scores, normalised over visible keys, rounded to bfloat16. `out_second`: likewise for the second pair. log_totals[h, 0] and log_totals[h, 1] are the logarithms of the sums over visible keys of exp of the first and second pair's scaled scores.
All inputs are finite; a program needn't handle non-finite values.
Results may differ from the reference program's by a relative error of at most 0.0085.
Values may be sent and summed in bfloat16 or wider, within the bound.
No kernel may reach another device: no remote copies, remote signals or barrier semaphores. Data moves between devices by JAX's collectives and lax.ppermute only.
A program may use at most 64 MiB of HBM per device.

```python
import math
import jax
import jax.numpy as jnp
from jax import lax

DH = 128
DV = 256
BLOCK = 64
HEADS = 2
N_BLK = 16


def paired_table(key):
    lower_block = jax.random.permutation(jax.random.fold_in(key, 11), N_BLK).astype(jnp.int32)
    upper_block = 2 * N_BLK - 1 - lower_block
    return jnp.stack([lower_block, upper_block], axis=1).reshape(2 * N_BLK)


def random_rows(key, label_id, feature_width):
    branch_key = jax.random.fold_in(key, label_id)
    shape_all = (2 * N_BLK, BLOCK, HEADS, feature_width)
    drawn_rows = jax.random.truncated_normal(jax.random.fold_in(branch_key, 1), -6.0, 6.0, shape_all, jnp.float32)
    return drawn_rows.astype(jnp.bfloat16)


def forward_pass(key, query_label, key_label):
    total_rows = 2 * N_BLK * BLOCK
    positions = (paired_table(key)[:, None] * BLOCK + jnp.arange(BLOCK, dtype=jnp.int32)[None, :]).reshape(total_rows)

    def heads_first(member):
        return jnp.transpose(member.reshape(total_rows, HEADS, member.shape[3]), (1, 0, 2)).astype(jnp.float32)
    queries = heads_first(random_rows(key, query_label, DH))
    keys_all = heads_first(random_rows(key, key_label, DH))
    values_all = heads_first(random_rows(key, 5, DV))
    tile_rows = min(512, total_rows)
    starts = jnp.arange(0, total_rows, tile_rows)

    def per_head(head_in):
        head_query, head_key, head_value = head_in

        def per_block(first_row):
            block_query = lax.dynamic_slice_in_dim(head_query, first_row, tile_rows, 0)
            block_pos = lax.dynamic_slice_in_dim(positions, first_row, tile_rows, 0)
            scores = jnp.dot(block_query, head_key.T, precision=lax.Precision.HIGHEST) / math.sqrt(DH)
            scores = jnp.where(positions[None, :] <= block_pos[:, None], scores, -jnp.inf)
            largest = jnp.max(scores, axis=1, keepdims=True)
            weights = jnp.exp(scores - largest)
            weight_sum = jnp.sum(weights, axis=1, keepdims=True)
            log_total = (largest + jnp.log(weight_sum))[:, 0]
            mixed_rows = jnp.dot(weights / weight_sum, head_value, precision=lax.Precision.HIGHEST)
            return (log_total, mixed_rows)
        log_total, mixed_rows = lax.map(per_block, starts)
        return (log_total.reshape(total_rows), mixed_rows.reshape(total_rows, DV))
    return lax.map(per_head, (queries, keys_all, values_all))


def rows_first(mixed_rows):
    return jnp.transpose(mixed_rows, (1, 0, 2)).reshape(2 * N_BLK, BLOCK, HEADS, DV).astype(jnp.bfloat16)


def draw_query_first(key, part):
    return random_rows(key, 1, DH)


def draw_query_second(key, part):
    return random_rows(key, 2, DH)


def draw_key_first(key, part):
    return random_rows(key, 3, DH)


def draw_key_second(key, part):
    return random_rows(key, 4, DH)


def draw_values(key, part):
    return random_rows(key, 5, DV)


def draw_out_first(key, part):
    log_total, mixed_rows = forward_pass(key, 1, 3)
    return rows_first(mixed_rows)


def draw_out_second(key, part):
    log_total, mixed_rows = forward_pass(key, 2, 4)
    return rows_first(mixed_rows)


def draw_log_totals(key, part):
    total_one, unused_one = forward_pass(key, 1, 3)
    total_two, unused_two = forward_pass(key, 2, 4)
    return jnp.stack([total_one, total_two], axis=1).reshape(HEADS, 2, 2 * N_BLK, BLOCK)


def draw_block_of(key, part):
    return paired_table(key)


def block_scale(own_key, extent, pieces, least, high):
    gain, own = 1.0, jax.random.fold_in(own_key, 6)
    for axis_at, blocks in pieces:
        heights = jnp.exp(jax.random.uniform(jax.random.fold_in(own, axis_at), (blocks,), jnp.float32, least / len(pieces), high / len(pieces)))
        gain = gain * jnp.repeat(heights, extent[axis_at] // blocks).reshape([-1 if axis == axis_at else 1 for axis in range(len(extent))])
    return gain


def bell_draw(key, shape, spread, most, pieces=(), held_as=jnp.bfloat16):
    array = jax.random.normal(key, shape, jnp.float32) * spread
    if len(pieces) > 0:
        array = block_scale(key, shape, pieces, -0.22, 0.18) * array
    return jnp.clip(array, min=-most, max=most).astype(held_as)


def setup_inputs(seed: int = 0) -> dict:
    seeds = jax.random.split(jax.random.key(seed), 13)
    query_first = draw_query_first(jax.random.fold_in(seeds[12], 71), 0)
    query_second = draw_query_second(jax.random.fold_in(seeds[12], 71), 0)
    key_first = draw_key_first(jax.random.fold_in(seeds[12], 71), 0)
    key_second = draw_key_second(jax.random.fold_in(seeds[12], 71), 0)
    values = draw_values(jax.random.fold_in(seeds[12], 71), 0)
    out_first = draw_out_first(jax.random.fold_in(seeds[12], 71), 0)
    out_second = draw_out_second(jax.random.fold_in(seeds[12], 71), 0)
    log_totals = draw_log_totals(jax.random.fold_in(seeds[12], 71), 0)
    lambdas = jnp.clip(jnp.exp(math.log(0.8) - 2.0794415 * jax.random.uniform(seeds[8], (HEADS,), jnp.float32) ** block_scale(seeds[8], (HEADS,), ((0, 2),), -0.2, 0.2)), 0.1, 0.8)
    norm_gain = jnp.clip(1.0 + 0.18 * jax.random.normal(seeds[9], (HEADS, DV), jnp.float32), 0.1, 1.9)
    cotangent = bell_draw(seeds[10], (2 * N_BLK, BLOCK, HEADS, DV), 1.0, 6.0, ((0, 16), (1, 2)))
    block_of = draw_block_of(jax.random.fold_in(seeds[12], 71), 0)
    return dict(query_first=query_first, query_second=query_second, key_first=key_first, key_second=key_second, values=values, out_first=out_first, out_second=out_second, log_totals=log_totals, lambdas=lambdas, norm_gain=norm_gain, cotangent=cotangent, block_of=block_of)


norm_eps = 1e-05

def head_backward(inputs_all, positions, scale_qk, tile_rows):
    first_query, second_query, first_key, second_key, values, grad_out, head_stats, lambda_one = inputs_all
    total_rows = first_query.shape[0]
    block_count = total_rows // tile_rows

    def blocks(member):
        return member.reshape((block_count, tile_rows) + member.shape[1:])

    def one_block(running, block_in):
        key_one, key_two, value_sum = running
        block_first, block_second, block_grad, block_stats, block_pos = block_in
        visible = positions[None, :] <= block_pos[:, None]
        score_one = jnp.dot(block_first, first_key.T, preferred_element_type=jnp.float32) * scale_qk
        score_two = jnp.dot(block_second, second_key.T, preferred_element_type=jnp.float32) * scale_qk
        prob_one = jnp.exp(jnp.where(visible, score_one - block_stats[0][:, None], -jnp.inf))
        prob_two = jnp.exp(jnp.where(visible, score_two - block_stats[1][:, None], -jnp.inf))
        grad_attn = jnp.dot(block_grad, values.T, preferred_element_type=jnp.float32)
        grad_one = (prob_one * (grad_attn - block_stats[2][:, None])).astype(jnp.bfloat16)
        grad_two = (-lambda_one * prob_two * (grad_attn - block_stats[3][:, None])).astype(jnp.bfloat16)
        weights = (prob_one - lambda_one * prob_two).astype(jnp.bfloat16)
        query_one = (jnp.dot(grad_one, first_key, preferred_element_type=jnp.float32) * scale_qk).astype(jnp.bfloat16)
        query_two = (jnp.dot(grad_two, second_key, preferred_element_type=jnp.float32) * scale_qk).astype(jnp.bfloat16)
        key_one = key_one + jnp.dot(grad_one.T, block_first, preferred_element_type=jnp.float32)
        key_two = key_two + jnp.dot(grad_two.T, block_second, preferred_element_type=jnp.float32)
        value_sum = value_sum + jnp.dot(weights.T, block_grad, preferred_element_type=jnp.float32)
        return ((key_one, key_two, value_sum), (query_one, query_two))
    stats_blocks = jnp.transpose(head_stats.reshape(4, block_count, tile_rows), (1, 0, 2))
    zero_key = jnp.zeros((total_rows, first_key.shape[1]), jnp.float32)
    zero_value = jnp.zeros((total_rows, values.shape[1]), jnp.float32)
    finals, query_parts = lax.scan(one_block, (zero_key, zero_key, zero_value), (blocks(first_query), blocks(second_query), blocks(grad_out), stats_blocks, blocks(positions)))
    return (query_parts[0].reshape(total_rows, first_key.shape[1]), query_parts[1].reshape(total_rows, first_key.shape[1]), (finals[0] * scale_qk).astype(jnp.bfloat16), (finals[1] * scale_qk).astype(jnp.bfloat16), finals[2].astype(jnp.bfloat16))

def reference(query_first, query_second, key_first, key_second, values, out_first, out_second, log_totals, lambdas, norm_gain, cotangent, block_of):
    slot_count, block_len, head_count, key_width = query_first.shape
    total_rows = slot_count * block_len
    scale_qk = 1.0 / math.sqrt(key_width)
    positions = (block_of[:, None] * block_len + jnp.arange(block_len, dtype=jnp.int32)[None, :]).reshape(total_rows).astype(jnp.int32)
    first_out = out_first.astype(jnp.float32)
    second_out = out_second.astype(jnp.float32)
    combined = first_out - lambdas[None, None, :, None] * second_out
    inv_rms = lax.rsqrt(lax.optimization_barrier(jnp.mean(combined * combined, axis=-1, keepdims=True)) + norm_eps)
    gained = norm_gain[None, None] * cotangent.astype(jnp.float32)
    centre = lax.optimization_barrier(jnp.mean(combined * gained, axis=-1, keepdims=True))
    grad_out = (inv_rms * (gained - combined * inv_rms * inv_rms * centre)).astype(jnp.bfloat16)
    grad_wide = grad_out.astype(jnp.float32)
    dot_one = lax.optimization_barrier(jnp.sum(grad_wide * first_out, axis=-1)).reshape(total_rows, head_count).T
    dot_two = lax.optimization_barrier(jnp.sum(grad_wide * second_out, axis=-1)).reshape(total_rows, head_count).T
    head_stats = jnp.concatenate([log_totals.reshape(head_count, 2, total_rows), dot_one[:, None], dot_two[:, None]], axis=1)

    def heads_first(member):
        return jnp.transpose(member.reshape((total_rows, head_count) + member.shape[3:]), (1, 0, 2))
    tile_rows = min(512, total_rows)
    results = lax.map(lambda inputs_all: head_backward(inputs_all, positions, scale_qk, tile_rows), (heads_first(query_first), heads_first(query_second), heads_first(key_first), heads_first(key_second), heads_first(values), heads_first(grad_out), head_stats, lambdas))

    def rows_first(member):
        return jnp.transpose(member, (1, 0, 2)).reshape((slot_count, block_len, head_count, member.shape[2]))
    return (rows_first(results[0]), rows_first(results[1]), rows_first(results[2]), rows_first(results[3]), rows_first(results[4]))
```

```python
import functools
import math

import jax
import jax.numpy as jnp
from jax import lax
from jax.experimental import pallas as pl
from jax.experimental.pallas import tpu as pltpu
from jax.sharding import PartitionSpec as P

norm_eps = 1e-05
VMEM = pltpu.VMEM
SMEM = pltpu.SMEM
f32 = jnp.float32
bf16 = jnp.bfloat16


def span(bits):
    masks = [0]
    for bit in bits:
        masks = masks + [mask ^ bit for mask in masks]
    return masks


def group_bits(shards):
    width = shards.bit_length() - 1
    bits = [1 << place for place in range(width)]
    middle = bits[1:-1]
    take = (width + 1) // 2
    key_bits = middle[:take]
    query_bits = [bit for bit in bits[::-1] if bit not in key_bits]
    return query_bits, key_bits


def send(member, mask, shards):
    return lax.ppermute(member, "blk", [(place, place ^ mask) for place in range(shards)])


def in_vmem(count):
    return [pl.BlockSpec(memory_space=VMEM)] * count


def in_smem(count):
    return [pl.BlockSpec(memory_space=SMEM)] * count


def three_parts(exact):
    high = exact.astype(bf16)
    rest = exact - high.astype(f32)
    middle = rest.astype(bf16)
    low = (rest - middle.astype(f32)).astype(bf16)
    return high, middle, low


def grad_out_kernel(place, lam, own_ref, other_ref, one_ref, two_ref, gain_ref, log_ref, pack_ref):
    rows, width = one_ref.shape
    slots, half, _ = own_ref.shape
    own = own_ref[...].astype(f32)
    other = other_ref[...].astype(f32)
    first = place[0] == 0
    upper = jnp.where(first, own, other)
    lower = jnp.where(first, other, own)
    grad_y = jnp.concatenate([upper, lower], axis=1).reshape(rows, width)
    one = one_ref[...].astype(f32)
    two = two_ref[...].astype(f32)
    combined = one - lam[0] * two
    inv_rms = lax.rsqrt(jnp.mean(combined * combined, axis=1, keepdims=True) + norm_eps)
    gained = gain_ref[...] * grad_y
    centre = jnp.mean(combined * gained, axis=1, keepdims=True)
    grad_out = (inv_rms * (gained - combined * inv_rms * inv_rms * centre)).astype(bf16)
    pack_ref[:rows, :] = grad_out
    wide = grad_out.astype(f32)

    def as_row(column):
        return jnp.transpose(jnp.broadcast_to(column, (rows, rows)))[:1, :]

    dot_one = as_row(jnp.sum(wide * one, axis=1, keepdims=True))
    dot_two = as_row(jnp.sum(wide * two, axis=1, keepdims=True))
    logs = log_ref[...]
    wide_logs = jnp.concatenate([logs[0:1, :], logs[1:2, :]], axis=1)
    wide_dots = jnp.concatenate([dot_one, dot_two], axis=1)
    parts = three_parts(wide_logs) + three_parts(wide_dots)
    filler = jnp.zeros((pack_ref.shape[0] - rows - len(parts), width), f32)
    pack_ref[rows:, :] = jnp.concatenate([part.astype(f32) for part in parts] + [filler], axis=0).astype(
        bf16
    )


def tile_kernel(scale, block_len, q_masks, k_masks, keep, table, me, lam, *refs):
    nq, nk = len(q_masks), len(k_masks)
    q_refs, refs = refs[:nq], refs[nq:]
    do_refs, refs = refs[:nq], refs[nq:]
    k_refs, refs = refs[:nk], refs[nk:]
    dq_keep, dq_send, dkv_own = refs[:3]
    dkv_out = refs[3:]
    rows = q_refs[0].shape[0]
    kw = q_refs[0].shape[1] // 2
    vw = do_refs[0].shape[1]
    lam0 = lam[0]

    def places(mask, axis):
        shard = jnp.bitwise_xor(me[0], mask)
        low = table[2 * shard] * block_len
        high = (table[2 * shard + 1] - 1) * block_len
        shape = (rows, 1) if axis == 0 else (1, rows)
        offset = lax.broadcasted_iota(jnp.int32, shape, axis)
        return offset + jnp.where(offset < block_len, low, high)

    contract = (((1,), (1,)), ((), ()))
    along_keys = (((0,), (0,)), ((), ()))
    q_one = jnp.concatenate([ref[:, :kw] for ref in q_refs], axis=0)
    q_two = jnp.concatenate([ref[:, kw:] for ref in q_refs], axis=0)
    grad = jnp.concatenate([ref[:rows, :] for ref in do_refs], axis=0)
    q_pos = jnp.concatenate([places(mask, 1) for mask in q_masks], axis=1)

    def stat(row, side):
        pieces = []
        for ref in do_refs:
            block = ref[rows:, side * rows : (side + 1) * rows].astype(f32)
            pieces.append(block[row : row + 1] + block[row + 1 : row + 2] + block[row + 2 : row + 3])
        return jnp.concatenate(pieces, axis=1)

    log_one, log_two = stat(0, 0), stat(0, 1)
    dot_one, dot_two = stat(3, 0), stat(3, 1)
    dq_one = None
    dq_two = None
    for j, mask in enumerate(k_masks):
        k_one, k_two, val = k_refs[j][:, :kw], k_refs[j][:, kw : 2 * kw], k_refs[j][:, 2 * kw :]
        visible = places(mask, 0) <= q_pos
        s_one = lax.dot_general(k_one, q_one, contract, preferred_element_type=f32)
        s_two = lax.dot_general(k_two, q_two, contract, preferred_element_type=f32)
        d_attn = lax.dot_general(val, grad, contract, preferred_element_type=f32)
        p_one = jnp.exp(jnp.where(visible, s_one * scale - log_one, -jnp.inf))
        p_two = lam0 * jnp.exp(jnp.where(visible, s_two * scale - log_two, -jnp.inf))
        g_one = (p_one * (d_attn - dot_one)).astype(bf16)
        g_two = (p_two * (dot_two - d_attn)).astype(bf16)
        mix = (p_one - p_two).astype(bf16)
        dkv = dkv_own if mask == 0 else dkv_out[j - 1]
        dkv[:, :kw] = jnp.dot(g_one, q_one, preferred_element_type=f32).astype(dkv.dtype)
        dkv[:, kw : 2 * kw] = jnp.dot(g_two, q_two, preferred_element_type=f32).astype(dkv.dtype)
        dkv[:, 2 * kw :] = jnp.dot(mix, grad, preferred_element_type=f32).astype(dkv.dtype)
        one = lax.dot_general(g_one, k_one, along_keys, preferred_element_type=f32)
        two = lax.dot_general(g_two, k_two, along_keys, preferred_element_type=f32)
        dq_one = one if dq_one is None else dq_one + one
        dq_two = two if dq_two is None else dq_two + two
    kept = 0
    sent = 0
    for i, mask in enumerate(q_masks):
        part = slice(i * rows, (i + 1) * rows)
        if mask in keep:
            dq_keep[kept * rows : (kept + 1) * rows, :kw] = dq_one[part]
            dq_keep[kept * rows : (kept + 1) * rows, kw:] = dq_two[part]
            kept += 1
        else:
            dq_send[sent * rows : (sent + 1) * rows, :kw] = dq_one[part].astype(bf16)
            dq_send[sent * rows : (sent + 1) * rows, kw:] = dq_two[part].astype(bf16)
            sent += 1


def final_kernel(scale, count, dq_ref, dq_in, own_ref, *refs):
    dkv_in, outs = refs[:count], refs[count:]
    kw = outs[0].shape[1]
    dq = (dq_ref[...] + dq_in[...].astype(f32)) * scale
    outs[0][...] = dq[:, :kw].astype(bf16)
    outs[1][...] = dq[:, kw:].astype(bf16)
    total = own_ref[...]
    for ref in dkv_in:
        total = total + ref[...].astype(f32)
    outs[2][...] = (total[:, :kw] * scale).astype(bf16)
    outs[3][...] = (total[:, kw : 2 * kw] * scale).astype(bf16)
    outs[4][...] = total[:, 2 * kw :].astype(bf16)


def per_device(
    shards,
    ranks,
    query_first,
    query_second,
    key_first,
    key_second,
    values,
    out_first,
    out_second,
    log_totals,
    lambdas,
    norm_gain,
    cotangent,
    block_of,
):
    slot_count, block_len, heads_here, value_width = values.shape
    key_width = query_first.shape[3]
    rows = slot_count * block_len
    scale = 1.0 / math.sqrt(key_width)
    assert heads_here == 1 and slot_count == 2 and shards == 1 << (shards.bit_length() - 1)
    q_bits, k_bits = group_bits(shards)
    me = lax.axis_index("blk")
    rank = lax.axis_index("ulysses")
    me_one = me.reshape(1).astype(jnp.int32)

    def flat(member):
        return member.reshape(rows, member.shape[3])

    if ranks == 2:
        other = lax.dynamic_index_in_dim(cotangent, 1 - rank, axis=2, keepdims=False)
        own_half = lax.dynamic_index_in_dim(cotangent, rank, axis=2, keepdims=False)
        other_half = lax.ppermute(other, "ulysses", [(0, 1), (1, 0)])
        place = rank.reshape(1).astype(jnp.int32)
    else:
        whole = lax.all_to_all(cotangent, "ulysses", split_axis=2, concat_axis=1, tiled=True)
        whole = whole.reshape(slot_count, block_len, value_width)
        own_half, other_half = whole[:, : block_len // 2], whole[:, block_len // 2 :]
        place = jnp.zeros((1,), jnp.int32)

    key_pack = jnp.concatenate([flat(key_first), flat(key_second), flat(values)], axis=1)
    query_pack = jnp.concatenate([flat(query_first), flat(query_second)], axis=1)
    k_masks = span(k_bits)
    keys = {0: key_pack}
    for mask in k_masks[:0:-1]:
        keys[mask] = send(key_pack, mask, shards)

    def spread(member):
        held = {0: member}
        for bit in q_bits:
            for mask in list(held):
                held[mask ^ bit] = send(held[mask], bit, shards)
        return held

    queries = spread(query_pack)
    pack_rows = rows + 16
    grad_pack = pl.pallas_call(
        grad_out_kernel,
        out_shape=jax.ShapeDtypeStruct((pack_rows, value_width), bf16),
        in_specs=in_smem(2) + in_vmem(6),
        out_specs=pl.BlockSpec(memory_space=VMEM),
        name="grad_out",
    )(
        place,
        lambdas,
        own_half,
        other_half,
        flat(out_first),
        flat(out_second),
        norm_gain,
        log_totals.reshape(2, rows),
    )
    grads = spread(grad_pack)

    q_masks = span(q_bits)
    last = q_bits[-1]
    keep = [mask for mask in q_masks if not mask & last]
    half_count = len(q_masks) // 2
    nk = len(k_masks)
    width = 2 * key_width + value_width
    tile_rows = rows * len(q_masks)
    results = pl.pallas_call(
        functools.partial(tile_kernel, scale, block_len, q_masks, k_masks, keep),
        out_shape=[
            jax.ShapeDtypeStruct((half_count * rows, 2 * key_width), f32),
            jax.ShapeDtypeStruct((half_count * rows, 2 * key_width), bf16),
            jax.ShapeDtypeStruct((rows, width), f32),
        ]
        + [jax.ShapeDtypeStruct((rows, width), bf16)] * (nk - 1),
        in_specs=in_smem(3) + in_vmem(2 * len(q_masks) + nk),
        out_specs=in_vmem(2 + nk),
        compiler_params=pltpu.CompilerParams(vmem_limit_bytes=56 << 20),
        name="tile",
    )(
        block_of,
        me_one,
        lambdas,
        *[queries[mask] for mask in q_masks],
        *[grads[mask] for mask in q_masks],
        *[keys[mask] for mask in k_masks],
    )
    dq_keep, dq_send, dkv_own = results[:3]
    dkv_parts = results[3:]
    dkv_in = [None] * (nk - 1)
    for j in range(nk - 1, 0, -1):
        dkv_in[j - 1] = send(dkv_parts[j - 1], k_masks[j], shards)
    arrived = send(dq_send, last, shards)
    kept = dq_keep + arrived.astype(f32)
    for bit in q_bits[-2::-1]:
        size = kept.shape[0] // 2
        if bit == q_bits[0]:
            dq_in = send(kept[size:].astype(bf16), bit, shards)
            kept = kept[:size]
        else:
            kept = kept[:size] + send(kept[size:].astype(bf16), bit, shards).astype(f32)
    outs = pl.pallas_call(
        functools.partial(final_kernel, scale, nk - 1),
        out_shape=[jax.ShapeDtypeStruct((rows, key_width), bf16)] * 4
        + [jax.ShapeDtypeStruct((rows, value_width), bf16)],
        in_specs=in_vmem(3 + nk - 1),
        out_specs=in_vmem(5),
        name="final",
    )(kept, dq_in, dkv_own, *dkv_in)
    return tuple(
        out.reshape(slot_count, block_len, heads_here, out.shape[1]) for out in outs
    )


def solution(mesh):
    rows_spec = P("blk", None, "ulysses", None)
    in_specs = (rows_spec,) * 7 + (
        P("ulysses", None, "blk", None),
        P("ulysses"),
        P("ulysses", None),
        P("blk", "ulysses", None, None),
        P(),
    )
    body = functools.partial(per_device, mesh.shape["blk"], mesh.shape["ulysses"])
    return jax.shard_map(
        body, mesh=mesh, in_specs=in_specs, out_specs=(rows_spec,) * 5, check_vma=False
    )
```

```python
import functools
import math

import jax
import jax.numpy as jnp
from jax import lax
from jax.experimental import pallas as pl
from jax.experimental.pallas import tpu as pltpu
from jax.sharding import PartitionSpec as P


norm_eps = 1e-05
VMEM = pltpu.VMEM
SMEM = pltpu.SMEM
f32 = jnp.float32
bf16 = jnp.bfloat16


def span(bits):
    masks = [0]
    for bit in bits:
        masks = masks + [mask ^ bit for mask in masks]
    return masks


def group_bits(shards):
    width = shards.bit_length() - 1
    bits = [1 << place for place in range(width)]
    middle = bits[1:-1]
    take = (width + 1) // 2
    key_bits = middle[:take]
    query_bits = [bit for bit in bits[::-1] if bit not in key_bits]
    return query_bits, key_bits


def send(member, mask, shards):
    return lax.ppermute(member, "blk", [(place, place ^ mask) for place in range(shards)])


def in_vmem(count):
    return [pl.BlockSpec(memory_space=VMEM)] * count


def in_smem(count):
    return [pl.BlockSpec(memory_space=SMEM)] * count


def three_parts(exact):
    high = exact.astype(bf16)
    rest = exact - high.astype(f32)
    middle = rest.astype(bf16)
    low = (rest - middle.astype(f32)).astype(bf16)
    return high, middle, low


def grad_out_kernel(place, lam, own_ref, other_ref, one_ref, two_ref, gain_ref, log_ref, pack_ref):
    rows, width = one_ref.shape
    first = place[0] == 0
    own = jnp.where(first, own_ref[:, :, 0, :].astype(f32), own_ref[:, :, 1, :].astype(f32))
    other = jnp.where(first, other_ref[:, :, 0, :].astype(f32), other_ref[:, :, 1, :].astype(f32))
    upper = jnp.where(first, own, other)
    lower = jnp.where(first, other, own)
    grad_y = jnp.concatenate([upper, lower], axis=1).reshape(rows, width)
    one = one_ref[...].astype(f32)
    two = two_ref[...].astype(f32)
    combined = one - lam[0] * two
    inv_rms = lax.rsqrt(jnp.mean(combined * combined, axis=1, keepdims=True) + norm_eps)
    gained = gain_ref[...] * grad_y
    centre = jnp.mean(combined * gained, axis=1, keepdims=True)
    grad_out = (inv_rms * (gained - combined * inv_rms * inv_rms * centre)).astype(bf16)
    pack_ref[:rows, :] = grad_out
    wide = grad_out.astype(f32)

    def as_row(column):
        return jnp.transpose(jnp.broadcast_to(column, (rows, rows)))[:1, :]

    dot_one = as_row(jnp.sum(wide * one, axis=1, keepdims=True))
    dot_two = as_row(jnp.sum(wide * two, axis=1, keepdims=True))
    wide_logs = jnp.concatenate(
        [log_ref[side, slot : slot + 1, :] for side in range(2) for slot in range(log_ref.shape[1])], axis=1
    )
    wide_dots = jnp.concatenate([dot_one, dot_two], axis=1)
    parts = three_parts(wide_logs) + three_parts(wide_dots)
    filler = jnp.zeros((pack_ref.shape[0] - rows - len(parts), width), f32)
    pack_ref[rows:, :] = jnp.concatenate([part.astype(f32) for part in parts] + [filler], axis=0).astype(
        bf16
    )


def tile_kernel(scale, block_len, q_masks, k_masks, keep, table, me, lam, *refs):
    nq, nk = len(q_masks), len(k_masks)
    q_refs, refs = refs[:nq], refs[nq:]
    do_refs, refs = refs[:nq], refs[nq:]
    k_refs, refs = refs[:nk], refs[nk:]
    dq_keep, dq_send, dkv_own = refs[:3]
    dkv_out = refs[3:]
    rows = q_refs[0].shape[0]
    kw = q_refs[0].shape[1] // 2
    lam0 = lam[0]

    def places(mask, axis):
        shard = jnp.bitwise_xor(me[0], mask)
        low = table[2 * shard] * block_len
        high = (table[2 * shard + 1] - 1) * block_len
        shape = (rows, 1) if axis == 0 else (1, rows)
        offset = lax.broadcasted_iota(jnp.int32, shape, axis)
        return offset + jnp.where(offset < block_len, low, high)

    contract = (((1,), (1,)), ((), ()))
    along_keys = (((0,), (0,)), ((), ()))
    q_one = jnp.concatenate([ref[:, :kw] for ref in q_refs], axis=0)
    q_two = jnp.concatenate([ref[:, kw:] for ref in q_refs], axis=0)
    grad = jnp.concatenate([ref[:rows, :] for ref in do_refs], axis=0)
    q_pos = jnp.concatenate([places(mask, 1) for mask in q_masks], axis=1)

    def stat(row, side):
        pieces = []
        for ref in do_refs:
            block = ref[rows:, side * rows : (side + 1) * rows].astype(f32)
            pieces.append(block[row : row + 1] + block[row + 1 : row + 2] + block[row + 2 : row + 3])
        return jnp.concatenate(pieces, axis=1)

    log_one, log_two = stat(0, 0), stat(0, 1)
    dot_one, dot_two = stat(3, 0), stat(3, 1)
    dq_one = None
    dq_two = None
    for j, mask in enumerate(k_masks):
        k_one, k_two, val = k_refs[j][:, :kw], k_refs[j][:, kw : 2 * kw], k_refs[j][:, 2 * kw :]
        visible = places(mask, 0) <= q_pos
        s_one = lax.dot_general(k_one, q_one, contract, preferred_element_type=f32)
        s_two = lax.dot_general(k_two, q_two, contract, preferred_element_type=f32)
        d_attn = lax.dot_general(val, grad, contract, preferred_element_type=f32)
        p_one = jnp.exp(jnp.where(visible, s_one * scale - log_one, -jnp.inf))
        p_two = lam0 * jnp.exp(jnp.where(visible, s_two * scale - log_two, -jnp.inf))
        g_one = (p_one * (d_attn - dot_one)).astype(bf16)
        g_two = (p_two * (dot_two - d_attn)).astype(bf16)
        mix = (p_one - p_two).astype(bf16)
        dkv = dkv_own if mask == 0 else dkv_out[j - 1]
        dkv[:, :kw] = jnp.dot(g_one, q_one, preferred_element_type=f32).astype(dkv.dtype)
        dkv[:, kw : 2 * kw] = jnp.dot(g_two, q_two, preferred_element_type=f32).astype(dkv.dtype)
        dkv[:, 2 * kw :] = jnp.dot(mix, grad, preferred_element_type=f32).astype(dkv.dtype)
        one = lax.dot_general(g_one, k_one, along_keys, preferred_element_type=f32)
        two = lax.dot_general(g_two, k_two, along_keys, preferred_element_type=f32)
        dq_one = one if dq_one is None else dq_one + one
        dq_two = two if dq_two is None else dq_two + two
    kept = 0
    sent = 0
    for i, mask in enumerate(q_masks):
        part = slice(i * rows, (i + 1) * rows)
        if mask in keep:
            dq_keep[kept * rows : (kept + 1) * rows, :kw] = dq_one[part]
            dq_keep[kept * rows : (kept + 1) * rows, kw:] = dq_two[part]
            kept += 1
        else:
            dq_send[sent * rows : (sent + 1) * rows, :kw] = dq_one[part].astype(bf16)
            dq_send[sent * rows : (sent + 1) * rows, kw:] = dq_two[part].astype(bf16)
            sent += 1


def final_kernel(scale, count, dq_ref, dq_in, own_ref, *refs):
    dkv_in, outs = refs[:count], refs[count:]
    kw = outs[0].shape[1]
    dq = (dq_ref[...] + dq_in[...].astype(f32)) * scale
    outs[0][...] = dq[:, :kw].astype(bf16)
    outs[1][...] = dq[:, kw:].astype(bf16)
    total = own_ref[...]
    for ref in dkv_in:
        total = total + ref[...].astype(f32)
    outs[2][...] = (total[:, :kw] * scale).astype(bf16)
    outs[3][...] = (total[:, kw : 2 * kw] * scale).astype(bf16)
    outs[4][...] = total[:, 2 * kw :].astype(bf16)


def one_device(
    shards,
    ranks,
    query_first,
    query_second,
    key_first,
    key_second,
    values,
    out_first,
    out_second,
    log_totals,
    lambdas,
    norm_gain,
    cotangent,
    block_of,
):
    slot_count, block_len, heads_here, value_width = values.shape
    key_width = query_first.shape[3]
    rows = slot_count * block_len
    scale = 1.0 / math.sqrt(key_width)
    assert heads_here == 1 and slot_count == 2 and shards == 1 << (shards.bit_length() - 1)
    q_bits, k_bits = group_bits(shards)
    me = lax.axis_index("blk")
    rank = lax.axis_index("ulysses")
    me_one = me.reshape(1).astype(jnp.int32)

    def flat(member):
        return member.reshape(rows, member.shape[3])

    if ranks == 2:
        own_half = cotangent
        other_half = lax.ppermute(cotangent, "ulysses", [(0, 1), (1, 0)])
        place = rank.reshape(1).astype(jnp.int32)
    else:
        whole = lax.all_to_all(cotangent, "ulysses", split_axis=2, concat_axis=1, tiled=True)
        whole = jnp.concatenate([whole, whole], axis=2)
        own_half, other_half = whole[:, : block_len // 2], whole[:, block_len // 2 :]
        place = jnp.zeros((1,), jnp.int32)

    key_pack = jnp.concatenate([flat(key_first), flat(key_second), flat(values)], axis=1)
    query_pack = jnp.concatenate([flat(query_first), flat(query_second)], axis=1)
    k_masks = span(k_bits)
    keys = {0: key_pack}
    for mask in k_masks[:0:-1]:
        keys[mask] = send(key_pack, mask, shards)

    def spread(member):
        held = {0: member}
        for bit in q_bits:
            for mask in list(held):
                held[mask ^ bit] = send(held[mask], bit, shards)
        return held

    queries = spread(query_pack)
    pack_rows = rows + 16
    grad_pack = pl.pallas_call(
        grad_out_kernel,
        out_shape=jax.ShapeDtypeStruct((pack_rows, value_width), bf16),
        in_specs=in_smem(2) + in_vmem(6),
        out_specs=pl.BlockSpec(memory_space=VMEM),
        compiler_params=pltpu.CompilerParams(vmem_limit_bytes=4 << 20),
        name="grad_out",
    )(
        place,
        lambdas,
        own_half,
        other_half,
        flat(out_first),
        flat(out_second),
        norm_gain,
        log_totals.reshape(2, slot_count, block_len),
    )
    grads = spread(grad_pack)

    q_masks = span(q_bits)
    last = q_bits[-1]
    keep = [mask for mask in q_masks if not mask & last]
    half_count = len(q_masks) // 2
    nk = len(k_masks)
    width = 2 * key_width + value_width
    results = pl.pallas_call(
        functools.partial(tile_kernel, scale, block_len, q_masks, k_masks, keep),
        out_shape=[
            jax.ShapeDtypeStruct((half_count * rows, 2 * key_width), f32),
            jax.ShapeDtypeStruct((half_count * rows, 2 * key_width), bf16),
            jax.ShapeDtypeStruct((rows, width), f32),
        ]
        + [jax.ShapeDtypeStruct((rows, width), bf16)] * (nk - 1),
        in_specs=in_smem(3) + in_vmem(2 * len(q_masks) + nk),
        out_specs=in_vmem(2 + nk),
        compiler_params=pltpu.CompilerParams(vmem_limit_bytes=16 << 20),
        name="tile",
    )(
        block_of,
        me_one,
        lambdas,
        *[queries[mask] for mask in q_masks],
        *[grads[mask] for mask in q_masks],
        *[keys[mask] for mask in k_masks],
    )
    dq_keep, dq_send, dkv_own = results[:3]
    dkv_parts = results[3:]
    dkv_in = [None] * (nk - 1)
    for j in range(nk - 1, 0, -1):
        dkv_in[j - 1] = send(dkv_parts[j - 1], k_masks[j], shards)
    arrived = send(dq_send, last, shards)
    kept = dq_keep + arrived.astype(f32)
    for bit in q_bits[-2::-1]:
        size = kept.shape[0] // 2
        if bit == q_bits[0]:
            dq_in = send(kept[size:].astype(bf16), bit, shards)
            kept = kept[:size]
        else:
            kept = kept[:size] + send(kept[size:].astype(bf16), bit, shards).astype(f32)
    outs = pl.pallas_call(
        functools.partial(final_kernel, scale, nk - 1),
        out_shape=[jax.ShapeDtypeStruct((rows, key_width), bf16)] * 4
        + [jax.ShapeDtypeStruct((rows, value_width), bf16)],
        in_specs=in_vmem(3 + nk - 1),
        out_specs=in_vmem(5),
        compiler_params=pltpu.CompilerParams(vmem_limit_bytes=4 << 20),
        name="final",
    )(kept, dq_in, dkv_own, *dkv_in)
    return tuple(
        out.reshape(slot_count, block_len, heads_here, out.shape[1]) for out in outs
    )


def solution(mesh):
    rows_spec = P("blk", None, "ulysses", None)
    in_specs = (rows_spec,) * 7 + (
        P("ulysses", None, "blk", None),
        P("ulysses"),
        P("ulysses", None),
        P("blk", "ulysses", None, None),
        P(),
    )
    shards = mesh.shape["blk"]
    body = functools.partial(one_device, shards, mesh.shape["ulysses"])
    return jax.shard_map(
        body, mesh=mesh, in_specs=in_specs, out_specs=(rows_spec,) * 5, check_vma=False
    )
```

```python
import functools
import math

import jax
import jax.numpy as jnp
from jax import lax
from jax.experimental import pallas as pl
from jax.experimental.pallas import tpu as pltpu
from jax.sharding import PartitionSpec as P


norm_eps = 1e-05
VMEM = pltpu.VMEM
SMEM = pltpu.SMEM
f32 = jnp.float32
bf16 = jnp.bfloat16


def span(bits):
    masks = [0]
    for bit in bits:
        masks = masks + [mask ^ bit for mask in masks]
    return masks


def group_bits(shards):
    width = shards.bit_length() - 1
    bits = [1 << place for place in range(width)]
    middle = bits[1:-1]
    take = (width + 1) // 2
    key_bits = middle[:take]
    query_bits = [bit for bit in bits[::-1] if bit not in key_bits]
    return query_bits, key_bits


def send(member, mask, shards):
    return lax.ppermute(member, "blk", [(place, place ^ mask) for place in range(shards)])


def in_vmem(count):
    return [pl.BlockSpec(memory_space=VMEM)] * count


def in_smem(count):
    return [pl.BlockSpec(memory_space=SMEM)] * count


def three_parts(exact):
    high = exact.astype(bf16)
    rest = exact - high.astype(f32)
    middle = rest.astype(bf16)
    low = (rest - middle.astype(f32)).astype(bf16)
    return high, middle, low


def prepare_kernel(block_len, q_masks, k_masks, me, *refs):
    sources, (key_pack, query_pack, small, q_pos, k_pos) = refs[:8], refs[8:13]
    table, gain, logs, sems = refs[13:]
    rows, kw = sources[0].shape
    targets = [
        key_pack.at[:, :kw],
        key_pack.at[:, kw : 2 * kw],
        key_pack.at[:, 2 * kw :],
        query_pack.at[:, :kw],
        query_pack.at[:, kw:],
        gain,
        logs,
        table,
    ]
    copies = [
        pltpu.make_async_copy(source, target, sems.at[i])
        for i, (source, target) in enumerate(zip(sources, targets))
    ]
    for copy in copies[::-1]:
        copy.start()
    copies[7].wait()

    def places(mask, axis):
        shard = jnp.bitwise_xor(me[0], mask)
        low = table[2 * shard] * block_len
        high = (table[2 * shard + 1] - 1) * block_len
        shape = (rows, 1) if axis == 0 else (1, rows)
        offset = lax.broadcasted_iota(jnp.int32, shape, axis)
        return offset + jnp.where(offset < block_len, low, high)

    q_pos[...] = jnp.concatenate([places(mask, 1) for mask in q_masks], axis=1)
    for j, mask in enumerate(k_masks):
        k_pos[j * rows : (j + 1) * rows, :] = places(mask, 0)
    for copy in copies[:7]:
        copy.wait()
    width = gain.shape[1]
    wide_logs = jnp.concatenate(
        [logs[side, slot : slot + 1, :] for side in range(2) for slot in range(logs.shape[1])], axis=1
    )
    filler = jnp.zeros((small.shape[0] - 2, width), f32)
    small[...] = jnp.concatenate([gain[...], wide_logs, filler], axis=0)


def grad_out_kernel(place, lam, small, own_ref, other_ref, one_ref, two_ref, pack_ref):
    rows, width = one_ref.shape
    first = place[0] == 0
    own = jnp.where(first, own_ref[:, :, 0, :].astype(f32), own_ref[:, :, 1, :].astype(f32))
    other = jnp.where(first, other_ref[:, :, 0, :].astype(f32), other_ref[:, :, 1, :].astype(f32))
    upper = jnp.where(first, own, other)
    lower = jnp.where(first, other, own)
    grad_y = jnp.concatenate([upper, lower], axis=1).reshape(rows, width)
    one = one_ref[...].astype(f32)
    two = two_ref[...].astype(f32)
    combined = one - lam[0] * two
    inv_rms = lax.rsqrt(jnp.mean(combined * combined, axis=1, keepdims=True) + norm_eps)
    gained = small[0:1, :] * grad_y
    centre = jnp.mean(combined * gained, axis=1, keepdims=True)
    grad_out = (inv_rms * (gained - combined * inv_rms * inv_rms * centre)).astype(bf16)
    pack_ref[:rows, :] = grad_out
    wide = grad_out.astype(f32)

    def as_row(column):
        return jnp.transpose(jnp.broadcast_to(column, (rows, rows)))[:1, :]

    dot_one = as_row(jnp.sum(wide * one, axis=1, keepdims=True))
    dot_two = as_row(jnp.sum(wide * two, axis=1, keepdims=True))
    wide_dots = jnp.concatenate([dot_one, dot_two], axis=1)
    parts = three_parts(small[1:2, :]) + three_parts(wide_dots)
    filler = jnp.zeros((pack_ref.shape[0] - rows - len(parts), width), f32)
    pack_ref[rows:, :] = jnp.concatenate([part.astype(f32) for part in parts] + [filler], axis=0).astype(
        bf16
    )


def query_side(q_refs, do_refs, q_pos):
    rows, kw = q_refs[0].shape[0], q_refs[0].shape[1] // 2

    def stat(row, side):
        pieces = []
        for ref in do_refs:
            block = ref[rows:, side * rows : (side + 1) * rows].astype(f32)
            pieces.append(block[row : row + 1] + block[row + 1 : row + 2] + block[row + 2 : row + 3])
        return jnp.concatenate(pieces, axis=1)

    return (
        jnp.concatenate([ref[:, :kw] for ref in q_refs], axis=0),
        jnp.concatenate([ref[:, kw:] for ref in q_refs], axis=0),
        jnp.concatenate([ref[:rows, :] for ref in do_refs], axis=0),
        stat(0, 0),
        stat(0, 1),
        stat(3, 0),
        stat(3, 1),
        q_pos,
    )


def tile_terms(scale, lam, queries, k_ref, k_pos):
    q_one, q_two, grad, log_one, log_two, dot_one, dot_two, q_pos = queries
    kw = q_one.shape[1]
    contract = (((1,), (1,)), ((), ()))
    along_keys = (((0,), (0,)), ((), ()))
    k_one, k_two, val = k_ref[:, :kw], k_ref[:, kw : 2 * kw], k_ref[:, 2 * kw :]
    visible = k_pos <= q_pos
    s_one = lax.dot_general(k_one, q_one, contract, preferred_element_type=f32)
    s_two = lax.dot_general(k_two, q_two, contract, preferred_element_type=f32)
    d_attn = lax.dot_general(val, grad, contract, preferred_element_type=f32)
    p_one = jnp.exp(jnp.where(visible, s_one * scale - log_one, -jnp.inf))
    p_two = lam * jnp.exp(jnp.where(visible, s_two * scale - log_two, -jnp.inf))
    g_one = (p_one * (d_attn - dot_one)).astype(bf16)
    g_two = (p_two * (dot_two - d_attn)).astype(bf16)
    mix = (p_one - p_two).astype(bf16)
    return (
        jnp.dot(g_one, q_one, preferred_element_type=f32),
        jnp.dot(g_two, q_two, preferred_element_type=f32),
        jnp.dot(mix, grad, preferred_element_type=f32),
        lax.dot_general(g_one, k_one, along_keys, preferred_element_type=f32),
        lax.dot_general(g_two, k_two, along_keys, preferred_element_type=f32),
    )


def put_key_terms(out, terms, before=None):
    kw = terms[0].shape[1]
    for part, term in zip((slice(0, kw), slice(kw, 2 * kw), slice(2 * kw, None)), terms):
        out[:, part] = (term if before is None else term + before[:, part]).astype(out.dtype)


def added(sums, terms):
    return terms if sums is None else tuple(a + b for a, b in zip(sums, terms))


def key_rows(k_pos, place, rows):
    return k_pos[place * rows : (place + 1) * rows, :]


def tile_early_kernel(scale, half, places, lam, q_pos, k_pos, *refs):
    q_refs, do_refs, refs = refs[:half], refs[half : 2 * half], refs[2 * half :]
    k_refs, (dq_sum, *dkv) = refs[: len(places)], refs[len(places) :]
    rows = q_refs[0].shape[0]
    queries = query_side(q_refs, do_refs, q_pos[:, : half * rows])
    sums = None
    for ref, place, out in zip(k_refs, places, dkv):
        terms = tile_terms(scale, lam[0], queries, ref, key_rows(k_pos, place, rows))
        put_key_terms(out, terms[:3])
        sums = added(sums, terms[3:])
    kw = sums[0].shape[1]
    dq_sum[:, :kw], dq_sum[:, kw:] = sums


def tile_far_kernel(scale, half, places, whole_places, lam, q_pos, k_pos, *refs):
    count = len(places)
    q_refs, do_refs, refs = refs[: 2 * half], refs[2 * half : 4 * half], refs[4 * half :]
    k_refs, refs = refs[:count], refs[count:]
    whole_refs, refs = refs[: len(whole_places)], refs[len(whole_places) :]
    before, (dq_before, dq_sum, *dkv) = refs[:count], refs[count:]
    rows, kw = q_refs[0].shape[0], q_refs[0].shape[1] // 2
    edge = half * rows
    late = query_side(q_refs[half:], do_refs[half:], q_pos[:, edge:])
    late_sums = None
    for ref, place, old, out in zip(k_refs, places, before, dkv):
        terms = tile_terms(scale, lam[0], late, ref, key_rows(k_pos, place, rows))
        put_key_terms(out, terms[:3], old)
        late_sums = added(late_sums, terms[3:])
    whole = query_side(q_refs, do_refs, q_pos[...])
    sums = None
    for ref, place, out in zip(whole_refs, whole_places, dkv[count:]):
        terms = tile_terms(scale, lam[0], whole, ref, key_rows(k_pos, place, rows))
        put_key_terms(out, terms[:3])
        sums = added(sums, terms[3:])
    one, two = sums
    dq_sum[:edge, :kw] = dq_before[:, :kw] + one[:edge]
    dq_sum[:edge, kw:] = dq_before[:, kw:] + two[:edge]
    dq_sum[edge:, :kw] = late_sums[0] + one[edge:]
    dq_sum[edge:, kw:] = late_sums[1] + two[edge:]


def tile_near_kernel(scale, half, keep, sent, lam, q_pos, k_pos, *refs):
    q_refs, do_refs, refs = refs[:half], refs[half : 2 * half], refs[2 * half :]
    k_ref, before, dq_sum, dq_keep, dq_send, dkv = refs
    rows, kw = q_refs[0].shape[0], q_refs[0].shape[1] // 2
    edge = half * rows
    late = query_side(q_refs, do_refs, q_pos[:, edge:])
    terms = tile_terms(scale, lam[0], late, k_ref, key_rows(k_pos, 0, rows))
    put_key_terms(dkv, terms[:3], before)
    for out, order in ((dq_keep, keep), (dq_send, sent)):
        for slot, i in enumerate(order):
            here = slice(slot * rows, (slot + 1) * rows)
            from_sum = slice(i * rows, (i + 1) * rows)
            for side, term in ((slice(0, kw), terms[3]), (slice(kw, None), terms[4])):
                total = dq_sum[from_sum, side]
                if i >= half:
                    total = total + term[i * rows - edge : (i + 1) * rows - edge]
                out[here, side] = total.astype(out.dtype)


def final_kernel(scale, count, dq_ref, dq_in, own_ref, *refs):
    dkv_in, outs = refs[:count], refs[count:]
    kw = outs[0].shape[1]
    dq = (dq_ref[...] + dq_in[...].astype(f32)) * scale
    outs[0][...] = dq[:, :kw].astype(bf16)
    outs[1][...] = dq[:, kw:].astype(bf16)
    total = own_ref[...]
    for ref in dkv_in:
        total = total + ref[...].astype(f32)
    outs[2][...] = (total[:, :kw] * scale).astype(bf16)
    outs[3][...] = (total[:, kw : 2 * kw] * scale).astype(bf16)
    outs[4][...] = total[:, 2 * kw :].astype(bf16)


def one_device(
    shards,
    ranks,
    query_first,
    query_second,
    key_first,
    key_second,
    values,
    out_first,
    out_second,
    log_totals,
    lambdas,
    norm_gain,
    cotangent,
    block_of,
):
    slot_count, block_len, heads_here, value_width = values.shape
    key_width = query_first.shape[3]
    rows = slot_count * block_len
    scale = 1.0 / math.sqrt(key_width)
    assert heads_here == 1 and slot_count == 2 and shards == 1 << (shards.bit_length() - 1)
    q_bits, k_bits = group_bits(shards)
    top = q_bits[-1]
    early_masks = [mask for mask in span(q_bits) if not mask & q_bits[0]]
    q_masks = early_masks + [mask ^ q_bits[0] for mask in early_masks]
    k_masks = span(k_bits)
    nq, nk = len(q_masks), len(k_masks)
    width = 2 * key_width + value_width
    me = lax.axis_index("blk").reshape(1).astype(jnp.int32)
    rank = lax.axis_index("ulysses").reshape(1).astype(jnp.int32)
    limits = pltpu.CompilerParams(vmem_limit_bytes=16 << 20)

    def flat(member):
        return member.reshape(rows, member.shape[3])

    if ranks == 2:
        own_half = cotangent
        other_half = lax.ppermute(cotangent, "ulysses", [(0, 1), (1, 0)])
    else:
        whole = lax.all_to_all(cotangent, "ulysses", split_axis=2, concat_axis=1, tiled=True)
        whole = jnp.concatenate([whole, whole], axis=2)
        own_half, other_half = whole[:, : block_len // 2], whole[:, block_len // 2 :]
        rank = jnp.zeros((1,), jnp.int32)

    key_pack, query_pack, small, q_pos, k_pos = pl.pallas_call(
        functools.partial(prepare_kernel, block_len, q_masks, k_masks),
        out_shape=[
            jax.ShapeDtypeStruct((rows, width), bf16),
            jax.ShapeDtypeStruct((rows, 2 * key_width), bf16),
            jax.ShapeDtypeStruct((8, value_width), f32),
            jax.ShapeDtypeStruct((1, nq * rows), jnp.int32),
            jax.ShapeDtypeStruct((nk * rows, 1), jnp.int32),
        ],
        in_specs=in_smem(1) + [pl.BlockSpec(memory_space=pltpu.HBM)] * 8,
        out_specs=in_vmem(5),
        scratch_shapes=[
            SMEM(block_of.shape, jnp.int32),
            VMEM((1, value_width), f32),
            VMEM((2, slot_count, block_len), f32),
            pltpu.SemaphoreType.DMA((8,)),
        ],
        compiler_params=limits,
        name="prepare",
    )(
        me,
        *[
            pltpu.with_memory_space_constraint(member, pltpu.HBM)
            for member in (
                flat(key_first),
                flat(key_second),
                flat(values),
                flat(query_first),
                flat(query_second),
                norm_gain,
                log_totals.reshape(2, slot_count, block_len),
                block_of,
            )
        ],
    )

    def spread(member, bits):
        held = {0: member}
        for bit in bits:
            for mask in list(held):
                held[mask ^ bit] = send(held[mask], bit, shards)
        return held

    keys = spread(key_pack, k_bits[::-1])
    queries = spread(query_pack, q_bits)
    grad_pack = pl.pallas_call(
        grad_out_kernel,
        out_shape=jax.ShapeDtypeStruct((rows + 16, value_width), bf16),
        in_specs=in_smem(2) + in_vmem(5),
        out_specs=pl.BlockSpec(memory_space=VMEM),
        compiler_params=limits,
        name="grad_out",
    )(rank, lambdas, small, own_half, other_half, flat(out_first), flat(out_second))
    grads = spread(grad_pack, q_bits)

    half = nq // 2
    keep_masks = [mask for mask in span(q_bits) if not mask & top]
    keep = [q_masks.index(mask) for mask in keep_masks]
    sent = [q_masks.index(mask ^ top) for mask in keep_masks]

    def query_parts(masks):
        return [queries[mask] for mask in masks] + [grads[mask] for mask in masks]

    def shape(row_count, columns, dtype):
        return jax.ShapeDtypeStruct((row_count, columns), dtype)

    def tile(kernel, outs, *operands):
        return pl.pallas_call(
            kernel,
            out_shape=outs,
            in_specs=in_smem(1) + in_vmem(2 + len(operands)),
            out_specs=in_vmem(len(outs)),
            compiler_params=limits,
        )(lambdas, q_pos, k_pos, *operands)

    early = [0] + [k_masks.index(k_bits[-1])]
    whole = [j for j in range(nk) if j not in early]
    far = early[1:] + whole
    dq_early, *early_parts = tile(
        functools.partial(tile_early_kernel, scale, half, early),
        [shape(half * rows, 2 * key_width, f32)] + [shape(rows, width, f32)] * len(early),
        *query_parts(q_masks[:half]),
        *[keys[k_masks[j]] for j in early],
    )
    dq_sum, *far_parts = tile(
        functools.partial(tile_far_kernel, scale, half, early[1:], whole),
        [shape(nq * rows, 2 * key_width, f32)] + [shape(rows, width, bf16)] * (nk - 1),
        *query_parts(q_masks),
        *[keys[k_masks[j]] for j in far],
        *early_parts[1:],
        dq_early,
    )
    dq_keep, dq_send, dkv_own = tile(
        functools.partial(tile_near_kernel, scale, half, keep, sent),
        [
            shape(half * rows, 2 * key_width, f32),
            shape(half * rows, 2 * key_width, bf16),
            shape(rows, width, f32),
        ],
        *query_parts(q_masks[half:]),
        key_pack,
        early_parts[0],
        dq_sum,
    )
    held = dict(zip(far, far_parts))
    dkv_in = [send(held[j], k_masks[j], shards) for j in range(1, nk)]
    arrived = send(dq_send, top, shards)
    kept = dq_keep + arrived.astype(f32)
    for bit in q_bits[-2::-1]:
        size = kept.shape[0] // 2
        dq_in = send(kept[size:].astype(bf16), bit, shards)
        kept = kept[:size]
        if bit != q_bits[0]:
            kept = kept + dq_in.astype(f32)
    outs = pl.pallas_call(
        functools.partial(final_kernel, scale, nk - 1),
        out_shape=[jax.ShapeDtypeStruct((rows, key_width), bf16)] * 4
        + [jax.ShapeDtypeStruct((rows, value_width), bf16)],
        in_specs=in_vmem(3 + nk - 1),
        out_specs=in_vmem(5),
        compiler_params=limits,
        name="final",
    )(kept, dq_in, dkv_own, *dkv_in)
    return tuple(
        out.reshape(slot_count, block_len, heads_here, out.shape[1]) for out in outs
    )


def solution(mesh):
    rows_spec = P("blk", None, "ulysses", None)
    in_specs = (rows_spec,) * 7 + (
        P("ulysses", None, "blk", None),
        P("ulysses"),
        P("ulysses", None),
        P("blk", "ulysses", None, None),
        P(),
    )
    shards = mesh.shape["blk"]
    body = functools.partial(one_device, shards, mesh.shape["ulysses"])
    return jax.shard_map(
        body, mesh=mesh, in_specs=in_specs, out_specs=(rows_spec,) * 5, check_vma=False
    )
```

```python
import functools
import math

import jax
import jax.numpy as jnp
from jax import lax
from jax.experimental import pallas as pl
from jax.experimental.pallas import tpu as pltpu
from jax.sharding import PartitionSpec as P


norm_eps = 1e-05
log2_e = math.log2(math.e)
VMEM = pltpu.VMEM
SMEM = pltpu.SMEM
f32 = jnp.float32
bf16 = jnp.bfloat16


def span(bits):
    masks = [0]
    for bit in bits:
        masks = masks + [mask ^ bit for mask in masks]
    return masks


def group_bits(shards):
    width = shards.bit_length() - 1
    bits = [1 << place for place in range(width)]
    middle = bits[1:-1]
    take = (width + 1) // 2
    key_bits = middle[:take]
    query_bits = [bit for bit in bits[::-1] if bit not in key_bits]
    return query_bits, key_bits


def send(member, mask, shards):
    return lax.ppermute(member, "blk", [(place, place ^ mask) for place in range(shards)])


def in_vmem(count):
    return [pl.BlockSpec(memory_space=VMEM)] * count


def in_smem(count):
    return [pl.BlockSpec(memory_space=SMEM)] * count


def three_parts(exact):
    high = exact.astype(bf16)
    rest = exact - high.astype(f32)
    middle = rest.astype(bf16)
    low = (rest - middle.astype(f32)).astype(bf16)
    return high, middle, low


def prepare_kernel(block_len, q_masks, k_masks, me, *refs):
    sources, (key_pack, query_pack, small, q_pos, k_pos) = refs[:8], refs[8:13]
    table, gain, logs, sems = refs[13:]
    rows, kw = sources[0].shape
    targets = [
        key_pack.at[:, :kw],
        key_pack.at[:, kw : 2 * kw],
        key_pack.at[:, 2 * kw :],
        query_pack.at[:, :kw],
        query_pack.at[:, kw:],
        gain,
        logs,
        table,
    ]
    copies = [
        pltpu.make_async_copy(source, target, sems.at[i])
        for i, (source, target) in enumerate(zip(sources, targets))
    ]
    for copy in copies[::-1]:
        copy.start()
    copies[7].wait()

    def places(mask, axis):
        shard = jnp.bitwise_xor(me[0], mask)
        low = table[2 * shard] * block_len
        high = (table[2 * shard + 1] - 1) * block_len
        shape = (rows, 1) if axis == 0 else (1, rows)
        offset = lax.broadcasted_iota(jnp.int32, shape, axis)
        return offset + jnp.where(offset < block_len, low, high)

    q_pos[...] = jnp.concatenate([places(mask, 1) for mask in q_masks], axis=1)
    for j, mask in enumerate(k_masks):
        k_pos[j * rows : (j + 1) * rows, :] = places(mask, 0)
    for copy in copies[:7]:
        copy.wait()
    width = gain.shape[1]
    wide_logs = jnp.concatenate(
        [logs[side, slot : slot + 1, :] for side in range(2) for slot in range(logs.shape[1])], axis=1
    )
    filler = jnp.zeros((small.shape[0] - 2, width), f32)
    small[...] = jnp.concatenate([gain[...], wide_logs, filler], axis=0)


def grad_out_kernel(place, lam, small, own_ref, other_ref, one_ref, two_ref, pack_ref):
    rows, width = one_ref.shape
    first = place[0] == 0
    own = jnp.where(first, own_ref[:, :, 0, :].astype(f32), own_ref[:, :, 1, :].astype(f32))
    other = jnp.where(first, other_ref[:, :, 0, :].astype(f32), other_ref[:, :, 1, :].astype(f32))
    upper = jnp.where(first, own, other)
    lower = jnp.where(first, other, own)
    grad_y = jnp.concatenate([upper, lower], axis=1).reshape(rows, width)
    one = one_ref[...].astype(f32)
    two = two_ref[...].astype(f32)
    combined = one - lam[0] * two
    inv_rms = lax.rsqrt(jnp.mean(combined * combined, axis=1, keepdims=True) + norm_eps)
    gained = small[0:1, :] * grad_y
    centre = jnp.mean(combined * gained, axis=1, keepdims=True)
    grad_out = (inv_rms * (gained - combined * inv_rms * inv_rms * centre)).astype(bf16)
    pack_ref[:rows, :] = grad_out
    wide = grad_out.astype(f32)

    def as_row(column):
        return jnp.transpose(jnp.broadcast_to(column, (rows, rows)))[:1, :]

    dot_one = as_row(jnp.sum(wide * one, axis=1, keepdims=True))
    dot_two = as_row(jnp.sum(wide * two, axis=1, keepdims=True))
    wide_dots = jnp.concatenate([dot_one, dot_two], axis=1)
    parts = three_parts(small[1:2, :]) + three_parts(wide_dots)
    filler = jnp.zeros((pack_ref.shape[0] - rows - len(parts), width), f32)
    pack_ref[rows:, :] = jnp.concatenate([part.astype(f32) for part in parts] + [filler], axis=0).astype(
        bf16
    )


def query_side(scale, lam, q_refs, do_refs, q_pos):
    rows, kw = q_refs[0].shape[0], q_refs[0].shape[1] // 2

    def stat(row, side):
        pieces = []
        for ref in do_refs:
            block = ref[rows:, side * rows : (side + 1) * rows].astype(f32)
            pieces.append(block[row : row + 1] + block[row + 1 : row + 2] + block[row + 2 : row + 3])
        return jnp.concatenate(pieces, axis=1)

    log_one = stat(0, 0) * -log2_e
    log_two = stat(0, 1) * -log2_e
    return (
        jnp.concatenate([ref[:, :kw] for ref in q_refs], axis=0),
        jnp.concatenate([ref[:, kw:] for ref in q_refs], axis=0),
        jnp.concatenate([ref[:rows, :] for ref in do_refs], axis=0),
        scale * log2_e,
        log_one,
        log_two + jnp.log(jnp.full(log_two.shape, lam, f32)) * log2_e,
        stat(3, 0),
        stat(3, 1),
        q_pos,
    )


def tile_terms(queries, k_refs, k_poss, own=False):
    q_one, q_two, grad, factor, log_one, log_two, dot_one, dot_two, q_pos = queries
    kw = q_one.shape[1]
    rows = k_refs[0].shape[0]
    contract = (((1,), (1,)), ((), ()))
    along_keys = (((0,), (0,)), ((), ()))
    k_one = jnp.concatenate([ref[:, :kw] for ref in k_refs], axis=0)
    k_two = jnp.concatenate([ref[:, kw : 2 * kw] for ref in k_refs], axis=0)
    val = jnp.concatenate([ref[:, 2 * kw :] for ref in k_refs], axis=0)
    s_one = lax.dot_general(k_one, q_one, contract, preferred_element_type=f32)
    s_two = lax.dot_general(k_two, q_two, contract, preferred_element_type=f32)
    d_attn = lax.dot_general(val, grad, contract, preferred_element_type=f32)

    def weights(score, log):
        score = score * factor
        parts = []
        for i, k_pos in enumerate(k_poss):
            if own and i == 0:
                seen = jnp.where(k_pos <= q_pos, score[:rows] + log, -jnp.inf)
                parts.append(jnp.exp2(seen))
                continue
            for first in (0, rows // 2):
                block = score[i * rows + first : i * rows + first + rows // 2]
                shift = jnp.where(k_pos[first : first + 1, :] <= q_pos, log, -jnp.inf)
                parts.append(jnp.exp2(block + shift))
        return jnp.concatenate(parts, axis=0)

    p_one = weights(s_one, log_one)
    p_two = weights(s_two, log_two)
    g_one = (p_one * (d_attn - dot_one)).astype(bf16)
    g_two = (p_two * (dot_two - d_attn)).astype(bf16)
    mix = (p_one - p_two).astype(bf16)
    return (
        jnp.dot(g_one, q_one, preferred_element_type=f32),
        jnp.dot(g_two, q_two, preferred_element_type=f32),
        jnp.dot(mix, grad, preferred_element_type=f32),
        lax.dot_general(g_one, k_one, along_keys, preferred_element_type=f32),
        lax.dot_general(g_two, k_two, along_keys, preferred_element_type=f32),
    )


def put_key_terms(outs, terms, befores=None):
    kw = terms[0].shape[1]
    for part, stacked in zip((slice(0, kw), slice(kw, 2 * kw), slice(2 * kw, None)), terms):
        for i, out in enumerate(outs):
            term = stacked[i * out.shape[0] : (i + 1) * out.shape[0]]
            out[:, part] = (term if befores is None else term + befores[i][:, part]).astype(out.dtype)


def key_rows(k_pos, place, rows):
    return k_pos[place * rows : (place + 1) * rows, :]


def tile_early_kernel(scale, half, places, lam, q_pos, k_pos, *refs):
    q_refs, do_refs, refs = refs[:half], refs[half : 2 * half], refs[2 * half :]
    k_refs, (dq_sum, *dkv) = refs[: len(places)], refs[len(places) :]
    rows = q_refs[0].shape[0]
    queries = query_side(scale, lam[0], q_refs, do_refs, q_pos[:, : half * rows])
    terms = tile_terms(queries, k_refs, [key_rows(k_pos, place, rows) for place in places], True)
    put_key_terms(dkv, terms[:3])
    kw = terms[3].shape[1]
    dq_sum[:, :kw], dq_sum[:, kw:] = terms[3:]


def tile_far_kernel(scale, half, places, whole_places, lam, q_pos, k_pos, *refs):
    count = len(places)
    q_refs, do_refs, refs = refs[: 2 * half], refs[2 * half : 4 * half], refs[4 * half :]
    k_refs, refs = refs[:count], refs[count:]
    whole_refs, refs = refs[: len(whole_places)], refs[len(whole_places) :]
    before, (dq_before, dq_sum, *dkv) = refs[:count], refs[count:]
    rows, kw = q_refs[0].shape[0], q_refs[0].shape[1] // 2
    edge = half * rows
    late = query_side(scale, lam[0], q_refs[half:], do_refs[half:], q_pos[:, edge:])
    terms = tile_terms(late, k_refs, [key_rows(k_pos, place, rows) for place in places])
    put_key_terms(dkv[:count], terms[:3], before)
    late_sums = terms[3:]
    whole = query_side(scale, lam[0], q_refs, do_refs, q_pos[...])
    terms = tile_terms(whole, whole_refs, [key_rows(k_pos, place, rows) for place in whole_places])
    put_key_terms(dkv[count:], terms[:3])
    one, two = terms[3:]
    dq_sum[:edge, :kw] = dq_before[:, :kw] + one[:edge]
    dq_sum[:edge, kw:] = dq_before[:, kw:] + two[:edge]
    dq_sum[edge:, :kw] = late_sums[0] + one[edge:]
    dq_sum[edge:, kw:] = late_sums[1] + two[edge:]


def tile_near_kernel(scale, half, keep, sent, lam, q_pos, k_pos, *refs):
    q_refs, do_refs, refs = refs[:half], refs[half : 2 * half], refs[2 * half :]
    k_ref, before, dq_sum, dq_keep, dq_send, dkv = refs
    rows, kw = q_refs[0].shape[0], q_refs[0].shape[1] // 2
    edge = half * rows
    late = query_side(scale, lam[0], q_refs, do_refs, q_pos[:, edge:])
    terms = tile_terms(late, [k_ref], [key_rows(k_pos, 0, rows)])
    put_key_terms([dkv], terms[:3], [before])
    for out, order in ((dq_keep, keep), (dq_send, sent)):
        for slot, i in enumerate(order):
            here = slice(slot * rows, (slot + 1) * rows)
            from_sum = slice(i * rows, (i + 1) * rows)
            for side, term in ((slice(0, kw), terms[3]), (slice(kw, None), terms[4])):
                total = dq_sum[from_sum, side]
                if i >= half:
                    total = total + term[i * rows - edge : (i + 1) * rows - edge]
                out[here, side] = total.astype(out.dtype)


def final_kernel(scale, count, dq_ref, dq_in, own_ref, *refs):
    dkv_in, outs = refs[:count], refs[count:]
    kw = outs[0].shape[1]
    dq = (dq_ref[...] + dq_in[...].astype(f32)) * scale
    outs[0][...] = dq[:, :kw].astype(bf16)
    outs[1][...] = dq[:, kw:].astype(bf16)
    total = own_ref[...]
    for ref in dkv_in:
        total = total + ref[...].astype(f32)
    outs[2][...] = (total[:, :kw] * scale).astype(bf16)
    outs[3][...] = (total[:, kw : 2 * kw] * scale).astype(bf16)
    outs[4][...] = total[:, 2 * kw :].astype(bf16)


def one_device(
    shards,
    ranks,
    query_first,
    query_second,
    key_first,
    key_second,
    values,
    out_first,
    out_second,
    log_totals,
    lambdas,
    norm_gain,
    cotangent,
    block_of,
):
    slot_count, block_len, heads_here, value_width = values.shape
    key_width = query_first.shape[3]
    rows = slot_count * block_len
    scale = 1.0 / math.sqrt(key_width)
    assert heads_here == 1 and slot_count == 2 and shards == 1 << (shards.bit_length() - 1)
    q_bits, k_bits = group_bits(shards)
    top = q_bits[-1]
    early_masks = [mask for mask in span(q_bits) if not mask & q_bits[0]]
    q_masks = early_masks + [mask ^ q_bits[0] for mask in early_masks]
    k_masks = span(k_bits)
    nq, nk = len(q_masks), len(k_masks)
    width = 2 * key_width + value_width
    me = lax.axis_index("blk").reshape(1).astype(jnp.int32)
    rank = lax.axis_index("ulysses").reshape(1).astype(jnp.int32)
    limits = pltpu.CompilerParams(vmem_limit_bytes=16 << 20)

    def flat(member):
        return member.reshape(rows, member.shape[3])

    if ranks == 2:
        own_half = cotangent
        other_half = lax.ppermute(cotangent, "ulysses", [(0, 1), (1, 0)])
    else:
        whole = lax.all_to_all(cotangent, "ulysses", split_axis=2, concat_axis=1, tiled=True)
        whole = jnp.concatenate([whole, whole], axis=2)
        own_half, other_half = whole[:, : block_len // 2], whole[:, block_len // 2 :]
        rank = jnp.zeros((1,), jnp.int32)

    key_pack, query_pack, small, q_pos, k_pos = pl.pallas_call(
        functools.partial(prepare_kernel, block_len, q_masks, k_masks),
        out_shape=[
            jax.ShapeDtypeStruct((rows, width), bf16),
            jax.ShapeDtypeStruct((rows, 2 * key_width), bf16),
            jax.ShapeDtypeStruct((8, value_width), f32),
            jax.ShapeDtypeStruct((1, nq * rows), jnp.int32),
            jax.ShapeDtypeStruct((nk * rows, 1), jnp.int32),
        ],
        in_specs=in_smem(1) + [pl.BlockSpec(memory_space=pltpu.HBM)] * 8,
        out_specs=in_vmem(5),
        scratch_shapes=[
            SMEM(block_of.shape, jnp.int32),
            VMEM((1, value_width), f32),
            VMEM((2, slot_count, block_len), f32),
            pltpu.SemaphoreType.DMA((8,)),
        ],
        compiler_params=limits,
        name="prepare",
    )(
        me,
        *[
            pltpu.with_memory_space_constraint(member, pltpu.HBM)
            for member in (
                flat(key_first),
                flat(key_second),
                flat(values),
                flat(query_first),
                flat(query_second),
                norm_gain,
                log_totals.reshape(2, slot_count, block_len),
                block_of,
            )
        ],
    )

    def spread(member, bits):
        held = {0: member}
        for bit in bits:
            for mask in list(held):
                held[mask ^ bit] = send(held[mask], bit, shards)
        return held

    keys = spread(key_pack, k_bits[::-1])
    queries = spread(query_pack, q_bits)
    grad_pack = pl.pallas_call(
        grad_out_kernel,
        out_shape=jax.ShapeDtypeStruct((rows + 16, value_width), bf16),
        in_specs=in_smem(2) + in_vmem(5),
        out_specs=pl.BlockSpec(memory_space=VMEM),
        compiler_params=limits,
        name="grad_out",
    )(rank, lambdas, small, own_half, other_half, flat(out_first), flat(out_second))
    grads = spread(grad_pack, q_bits)

    half = nq // 2
    keep_masks = [mask for mask in span(q_bits) if not mask & top]
    keep = [q_masks.index(mask) for mask in keep_masks]
    sent = [q_masks.index(mask ^ top) for mask in keep_masks]

    def query_parts(masks):
        return [queries[mask] for mask in masks] + [grads[mask] for mask in masks]

    def shape(row_count, columns, dtype):
        return jax.ShapeDtypeStruct((row_count, columns), dtype)

    def tile(kernel, outs, *operands):
        return pl.pallas_call(
            kernel,
            out_shape=outs,
            in_specs=in_smem(1) + in_vmem(2 + len(operands)),
            out_specs=in_vmem(len(outs)),
            compiler_params=limits,
        )(lambdas, q_pos, k_pos, *operands)

    early = [0] + [k_masks.index(k_bits[-1])]
    whole = [j for j in range(nk) if j not in early]
    far = early[1:] + whole
    dq_early, *early_parts = tile(
        functools.partial(tile_early_kernel, scale, half, early),
        [shape(half * rows, 2 * key_width, f32)] + [shape(rows, width, f32)] * len(early),
        *query_parts(q_masks[:half]),
        *[keys[k_masks[j]] for j in early],
    )
    dq_sum, *far_parts = tile(
        functools.partial(tile_far_kernel, scale, half, early[1:], whole),
        [shape(nq * rows, 2 * key_width, f32)] + [shape(rows, width, bf16)] * (nk - 1),
        *query_parts(q_masks),
        *[keys[k_masks[j]] for j in far],
        *early_parts[1:],
        dq_early,
    )
    dq_keep, dq_send, dkv_own = tile(
        functools.partial(tile_near_kernel, scale, half, keep, sent),
        [
            shape(half * rows, 2 * key_width, f32),
            shape(half * rows, 2 * key_width, bf16),
            shape(rows, width, f32),
        ],
        *query_parts(q_masks[half:]),
        key_pack,
        early_parts[0],
        dq_sum,
    )
    held = dict(zip(far, far_parts))
    dkv_in = [send(held[j], k_masks[j], shards) for j in range(1, nk)]
    arrived = send(dq_send, top, shards)
    kept = dq_keep + arrived.astype(f32)
    for bit in q_bits[-2::-1]:
        size = kept.shape[0] // 2
        dq_in = send(kept[size:].astype(bf16), bit, shards)
        kept = kept[:size]
        if bit != q_bits[0]:
            kept = kept + dq_in.astype(f32)
    outs = pl.pallas_call(
        functools.partial(final_kernel, scale, nk - 1),
        out_shape=[jax.ShapeDtypeStruct((rows, key_width), bf16)] * 4
        + [jax.ShapeDtypeStruct((rows, value_width), bf16)],
        in_specs=in_vmem(3 + nk - 1),
        out_specs=in_vmem(5),
        compiler_params=limits,
        name="final",
    )(kept, dq_in, dkv_own, *dkv_in)
    return tuple(
        out.reshape(slot_count, block_len, heads_here, out.shape[1]) for out in outs
    )


def solution(mesh):
    rows_spec = P("blk", None, "ulysses", None)
    in_specs = (rows_spec,) * 7 + (
        P("ulysses", None, "blk", None),
        P("ulysses"),
        P("ulysses", None),
        P("blk", "ulysses", None, None),
        P(),
    )
    shards = mesh.shape["blk"]
    body = functools.partial(one_device, shards, mesh.shape["ulysses"])
    return jax.shard_map(
        body, mesh=mesh, in_specs=in_specs, out_specs=(rows_spec,) * 5, check_vma=False
    )
```

```python
import functools
import math

import jax
import jax.numpy as jnp
from jax import lax
from jax.experimental import pallas as pl
from jax.experimental.pallas import tpu as pltpu
from jax.sharding import PartitionSpec as P


norm_eps = 1e-05
log2_e = math.log2(math.e)
VMEM = pltpu.VMEM
SMEM = pltpu.SMEM
f32 = jnp.float32
bf16 = jnp.bfloat16


def span(bits):
    masks = [0]
    for bit in bits:
        masks = masks + [mask ^ bit for mask in masks]
    return masks


def group_bits(shards):
    width = shards.bit_length() - 1
    bits = [1 << place for place in range(width)]
    middle = bits[1:-1]
    take = (width + 1) // 2
    key_bits = middle[:take]
    query_bits = [bit for bit in bits[::-1] if bit not in key_bits]
    return query_bits, key_bits


def send(member, mask, shards):
    return lax.ppermute(member, "blk", [(place, place ^ mask) for place in range(shards)])


def in_vmem(count):
    return [pl.BlockSpec(memory_space=VMEM)] * count


def in_smem(count):
    return [pl.BlockSpec(memory_space=SMEM)] * count


def three_parts(exact):
    high = exact.astype(bf16)
    rest = exact - high.astype(f32)
    middle = rest.astype(bf16)
    low = (rest - middle.astype(f32)).astype(bf16)
    return high, middle, low


def prepare_kernel(block_len, q_masks, k_masks, me, *refs):
    sources, (key_pack, query_pack, small, q_pos, k_pos) = refs[:8], refs[8:13]
    table, gain, logs, sems = refs[13:]
    rows, kw = sources[0].shape
    targets = [
        key_pack.at[:, :kw],
        key_pack.at[:, kw : 2 * kw],
        key_pack.at[:, 2 * kw :],
        query_pack.at[:, :kw],
        query_pack.at[:, kw:],
        gain,
        logs,
        table,
    ]
    copies = [
        pltpu.make_async_copy(source, target, sems.at[i])
        for i, (source, target) in enumerate(zip(sources, targets))
    ]
    for copy in copies[::-1]:
        copy.start()
    copies[7].wait()

    def places(mask, axis):
        shard = jnp.bitwise_xor(me[0], mask)
        low = table[2 * shard] * block_len
        high = (table[2 * shard + 1] - 1) * block_len
        shape = (rows, 1) if axis == 0 else (1, rows)
        offset = lax.broadcasted_iota(jnp.int32, shape, axis)
        return offset + jnp.where(offset < block_len, low, high)

    q_pos[...] = jnp.concatenate([places(mask, 1) for mask in q_masks], axis=1)
    for j, mask in enumerate(k_masks):
        k_pos[j * rows : (j + 1) * rows, :] = places(mask, 0)
    for copy in copies[:7]:
        copy.wait()
    width = gain.shape[1]
    wide_logs = jnp.concatenate(
        [logs[side, slot : slot + 1, :] for side in range(2) for slot in range(logs.shape[1])], axis=1
    )
    filler = jnp.zeros((small.shape[0] - 2, width), f32)
    small[...] = jnp.concatenate([gain[...], wide_logs, filler], axis=0)


def grad_out_kernel(place, lam, small, own_ref, other_ref, one_ref, two_ref, pack_ref):
    rows, width = one_ref.shape
    first = place[0] == 0
    own = jnp.where(first, own_ref[:, :, 0, :].astype(f32), own_ref[:, :, 1, :].astype(f32))
    other = jnp.where(first, other_ref[:, :, 0, :].astype(f32), other_ref[:, :, 1, :].astype(f32))
    upper = jnp.where(first, own, other)
    lower = jnp.where(first, other, own)
    grad_y = jnp.concatenate([upper, lower], axis=1).reshape(rows, width)
    one = one_ref[...].astype(f32)
    two = two_ref[...].astype(f32)
    combined = one - lam[0] * two
    inv_rms = lax.rsqrt(jnp.mean(combined * combined, axis=1, keepdims=True) + norm_eps)
    gained = small[0:1, :] * grad_y
    centre = jnp.mean(combined * gained, axis=1, keepdims=True)
    grad_out = (inv_rms * (gained - combined * inv_rms * inv_rms * centre)).astype(bf16)
    pack_ref[:rows, :] = grad_out
    wide = grad_out.astype(f32)

    def as_row(column):
        return jnp.transpose(jnp.broadcast_to(column, (rows, rows)))[:1, :]

    dot_one = as_row(jnp.sum(wide * one, axis=1, keepdims=True))
    dot_two = as_row(jnp.sum(wide * two, axis=1, keepdims=True))
    wide_dots = jnp.concatenate([dot_one, dot_two], axis=1)
    parts = three_parts(small[1:2, :]) + three_parts(wide_dots)
    filler = jnp.zeros((pack_ref.shape[0] - rows - len(parts), width), f32)
    pack_ref[rows:, :] = jnp.concatenate([part.astype(f32) for part in parts] + [filler], axis=0).astype(
        bf16
    )


def query_side(scale, lam, q_refs, do_refs, q_pos):
    rows, kw = q_refs[0].shape[0], q_refs[0].shape[1] // 2

    def stat(row, side):
        pieces = []
        for ref in do_refs:
            block = ref[rows:, side * rows : (side + 1) * rows].astype(f32)
            pieces.append(block[row : row + 1] + block[row + 1 : row + 2] + block[row + 2 : row + 3])
        return jnp.concatenate(pieces, axis=1)

    log_one = stat(0, 0) * -log2_e
    log_two = stat(0, 1) * -log2_e
    return (
        jnp.concatenate([ref[:, :kw] for ref in q_refs], axis=0),
        jnp.concatenate([ref[:, kw:] for ref in q_refs], axis=0),
        jnp.concatenate([ref[:rows, :] for ref in do_refs], axis=0),
        scale * log2_e,
        log_one,
        log_two + jnp.log(jnp.full(log_two.shape, lam, f32)) * log2_e,
        stat(3, 0),
        stat(3, 1),
        q_pos,
    )


def tile_terms(queries, k_refs, k_poss, own=False):
    q_one, q_two, grad, factor, log_one, log_two, dot_one, dot_two, q_pos = queries
    kw = q_one.shape[1]
    rows = k_refs[0].shape[0]
    contract = (((1,), (1,)), ((), ()))
    along_keys = (((0,), (0,)), ((), ()))
    k_one = jnp.concatenate([ref[:, :kw] for ref in k_refs], axis=0)
    k_two = jnp.concatenate([ref[:, kw : 2 * kw] for ref in k_refs], axis=0)
    val = jnp.concatenate([ref[:, 2 * kw :] for ref in k_refs], axis=0)
    s_one = lax.dot_general(k_one, q_one, contract, preferred_element_type=f32)
    s_two = lax.dot_general(k_two, q_two, contract, preferred_element_type=f32)
    d_attn = lax.dot_general(val, grad, contract, preferred_element_type=f32)

    def weights(score, log):
        score = score * factor
        parts = []
        for i, k_pos in enumerate(k_poss):
            if own and i == 0:
                seen = jnp.where(k_pos <= q_pos, score[:rows] + log, -jnp.inf)
                parts.append(jnp.exp2(seen))
                continue
            for first in (0, rows // 2):
                block = score[i * rows + first : i * rows + first + rows // 2]
                shift = jnp.where(k_pos[first : first + 1, :] <= q_pos, log, -jnp.inf)
                parts.append(jnp.exp2(block + shift))
        return jnp.concatenate(parts, axis=0)

    p_one = weights(s_one, log_one)
    p_two = weights(s_two, log_two)
    g_one = (p_one * (d_attn - dot_one)).astype(bf16)
    g_two = (p_two * (dot_two - d_attn)).astype(bf16)
    mix = (p_one - p_two).astype(bf16)
    return (
        jnp.dot(g_one, q_one, preferred_element_type=f32),
        jnp.dot(g_two, q_two, preferred_element_type=f32),
        jnp.dot(mix, grad, preferred_element_type=f32),
        lax.dot_general(g_one, k_one, along_keys, preferred_element_type=f32),
        lax.dot_general(g_two, k_two, along_keys, preferred_element_type=f32),
    )


def put_key_terms(outs, terms, befores=None):
    kw = terms[0].shape[1]
    for part, stacked in zip((slice(0, kw), slice(kw, 2 * kw), slice(2 * kw, None)), terms):
        for i, out in enumerate(outs):
            term = stacked[i * out.shape[0] : (i + 1) * out.shape[0]]
            out[:, part] = (term if befores is None else term + befores[i][:, part]).astype(out.dtype)


def key_rows(k_pos, place, rows):
    return k_pos[place * rows : (place + 1) * rows, :]


def tile_early_kernel(scale, half, places, lam, q_pos, k_pos, *refs):
    q_refs, do_refs, refs = refs[:half], refs[half : 2 * half], refs[2 * half :]
    k_refs, (dq_sum, *dkv) = refs[: len(places)], refs[len(places) :]
    rows = q_refs[0].shape[0]
    queries = query_side(scale, lam[0], q_refs, do_refs, q_pos[:, : half * rows])
    terms = tile_terms(queries, k_refs, [key_rows(k_pos, place, rows) for place in places], True)
    put_key_terms(dkv, terms[:3])
    kw = terms[3].shape[1]
    dq_sum[:, :kw], dq_sum[:, kw:] = terms[3:]


def tile_late_kernel(scale, half, places, whole_places, keep, sent, lam, q_pos, k_pos, *refs):
    count = len(places)
    q_refs, do_refs, refs = refs[: 2 * half], refs[2 * half : 4 * half], refs[4 * half :]
    k_refs, refs = refs[:count], refs[count:]
    whole_refs, refs = refs[: len(whole_places)], refs[len(whole_places) :]
    before, (dq_before, dq_keep, dq_send, *dkv) = refs[:count], refs[count:]
    rows, kw = q_refs[0].shape[0], q_refs[0].shape[1] // 2
    edge = half * rows
    late = query_side(scale, lam[0], q_refs[half:], do_refs[half:], q_pos[:, edge:])
    terms = tile_terms(late, k_refs, [key_rows(k_pos, place, rows) for place in places])
    put_key_terms(dkv[:count], terms[:3], before)
    late_sums = terms[3:]
    whole = query_side(scale, lam[0], q_refs, do_refs, q_pos[...])
    terms = tile_terms(whole, whole_refs, [key_rows(k_pos, place, rows) for place in whole_places])
    put_key_terms(dkv[count:], terms[:3])
    for out, order in ((dq_keep, keep), (dq_send, sent)):
        for slot, i in enumerate(order):
            here = slice(slot * rows, (slot + 1) * rows)
            for n, side in enumerate((slice(0, kw), slice(kw, None))):
                total = terms[3 + n][i * rows : (i + 1) * rows]
                if i < half:
                    total = total + dq_before[i * rows : (i + 1) * rows, side]
                else:
                    total = total + late_sums[n][i * rows - edge : (i + 1) * rows - edge]
                out[here, side] = total.astype(out.dtype)


def final_kernel(scale, count, dq_ref, dq_in, own_ref, *refs):
    dkv_in, outs = refs[:count], refs[count:]
    kw = outs[0].shape[1]
    dq = (dq_ref[...] + dq_in[...].astype(f32)) * scale
    outs[0][...] = dq[:, :kw].astype(bf16)
    outs[1][...] = dq[:, kw:].astype(bf16)
    total = own_ref[...]
    for ref in dkv_in:
        total = total + ref[...].astype(f32)
    outs[2][...] = (total[:, :kw] * scale).astype(bf16)
    outs[3][...] = (total[:, kw : 2 * kw] * scale).astype(bf16)
    outs[4][...] = total[:, 2 * kw :].astype(bf16)


def one_device(
    shards,
    ranks,
    query_first,
    query_second,
    key_first,
    key_second,
    values,
    out_first,
    out_second,
    log_totals,
    lambdas,
    norm_gain,
    cotangent,
    block_of,
):
    slot_count, block_len, heads_here, value_width = values.shape
    key_width = query_first.shape[3]
    rows = slot_count * block_len
    scale = 1.0 / math.sqrt(key_width)
    assert heads_here == 1 and slot_count == 2 and shards == 1 << (shards.bit_length() - 1)
    q_bits, k_bits = group_bits(shards)
    top = q_bits[-1]
    early_masks = [mask for mask in span(q_bits) if not mask & q_bits[0]]
    q_masks = early_masks + [mask ^ q_bits[0] for mask in early_masks]
    k_masks = span(k_bits)
    nq, nk = len(q_masks), len(k_masks)
    width = 2 * key_width + value_width
    me = lax.axis_index("blk").reshape(1).astype(jnp.int32)
    rank = lax.axis_index("ulysses").reshape(1).astype(jnp.int32)
    limits = pltpu.CompilerParams(vmem_limit_bytes=16 << 20)

    def flat(member):
        return member.reshape(rows, member.shape[3])

    if ranks == 2:
        own_half = cotangent
        other_half = lax.ppermute(cotangent, "ulysses", [(0, 1), (1, 0)])
    else:
        whole = lax.all_to_all(cotangent, "ulysses", split_axis=2, concat_axis=1, tiled=True)
        whole = jnp.concatenate([whole, whole], axis=2)
        own_half, other_half = whole[:, : block_len // 2], whole[:, block_len // 2 :]
        rank = jnp.zeros((1,), jnp.int32)

    key_pack, query_pack, small, q_pos, k_pos = pl.pallas_call(
        functools.partial(prepare_kernel, block_len, q_masks, k_masks),
        out_shape=[
            jax.ShapeDtypeStruct((rows, width), bf16),
            jax.ShapeDtypeStruct((rows, 2 * key_width), bf16),
            jax.ShapeDtypeStruct((8, value_width), f32),
            jax.ShapeDtypeStruct((1, nq * rows), jnp.int32),
            jax.ShapeDtypeStruct((nk * rows, 1), jnp.int32),
        ],
        in_specs=in_smem(1) + [pl.BlockSpec(memory_space=pltpu.HBM)] * 8,
        out_specs=in_vmem(5),
        scratch_shapes=[
            SMEM(block_of.shape, jnp.int32),
            VMEM((1, value_width), f32),
            VMEM((2, slot_count, block_len), f32),
            pltpu.SemaphoreType.DMA((8,)),
        ],
        compiler_params=limits,
        name="prepare",
    )(
        me,
        *[
            pltpu.with_memory_space_constraint(member, pltpu.HBM)
            for member in (
                flat(key_first),
                flat(key_second),
                flat(values),
                flat(query_first),
                flat(query_second),
                norm_gain,
                log_totals.reshape(2, slot_count, block_len),
                block_of,
            )
        ],
    )

    def spread(member, bits):
        held = {0: member}
        for bit in bits:
            for mask in list(held):
                held[mask ^ bit] = send(held[mask], bit, shards)
        return held

    keys = spread(key_pack, k_bits[::-1])
    queries = spread(query_pack, q_bits)
    grad_pack = pl.pallas_call(
        grad_out_kernel,
        out_shape=jax.ShapeDtypeStruct((rows + 8, value_width), bf16),
        in_specs=in_smem(2) + in_vmem(5),
        out_specs=pl.BlockSpec(memory_space=VMEM),
        compiler_params=limits,
        name="grad_out",
    )(rank, lambdas, small, own_half, other_half, flat(out_first), flat(out_second))
    grads = spread(grad_pack, q_bits)

    half = nq // 2
    keep_masks = [mask for mask in span(q_bits) if not mask & top]
    keep = [q_masks.index(mask) for mask in keep_masks]
    sent = [q_masks.index(mask ^ top) for mask in keep_masks]

    def query_parts(masks):
        return [queries[mask] for mask in masks] + [grads[mask] for mask in masks]

    def shape(row_count, columns, dtype):
        return jax.ShapeDtypeStruct((row_count, columns), dtype)

    def tile(kernel, outs, *operands):
        return pl.pallas_call(
            kernel,
            out_shape=outs,
            in_specs=in_smem(1) + in_vmem(2 + len(operands)),
            out_specs=in_vmem(len(outs)),
            compiler_params=limits,
        )(lambdas, q_pos, k_pos, *operands)

    early = [0] + [k_masks.index(k_bits[-1])]
    whole = [j for j in range(nk) if j not in early]
    far = early[1:] + whole
    dq_early, *early_parts = tile(
        functools.partial(tile_early_kernel, scale, half, early),
        [shape(half * rows, 2 * key_width, f32)] + [shape(rows, width, f32)] * len(early),
        *query_parts(q_masks[:half]),
        *[keys[k_masks[j]] for j in early],
    )
    dq_keep, dq_send, dkv_own, *far_parts = tile(
        functools.partial(tile_late_kernel, scale, half, early, whole, keep, sent),
        [
            shape(half * rows, 2 * key_width, f32),
            shape(half * rows, 2 * key_width, bf16),
            shape(rows, width, f32),
        ]
        + [shape(rows, width, bf16)] * (nk - 1),
        *query_parts(q_masks),
        *[keys[k_masks[j]] for j in early + whole],
        *early_parts,
        dq_early,
    )
    held = dict(zip(far, far_parts))
    dkv_in = [send(held[j], k_masks[j], shards) for j in range(1, nk)]
    arrived = send(dq_send, top, shards)
    kept = dq_keep + arrived.astype(f32)
    for bit in q_bits[-2::-1]:
        size = kept.shape[0] // 2
        dq_in = send(kept[size:].astype(bf16), bit, shards)
        kept = kept[:size]
        if bit != q_bits[0]:
            kept = kept + dq_in.astype(f32)
    outs = pl.pallas_call(
        functools.partial(final_kernel, scale, nk - 1),
        out_shape=[jax.ShapeDtypeStruct((rows, key_width), bf16)] * 4
        + [jax.ShapeDtypeStruct((rows, value_width), bf16)],
        in_specs=in_vmem(3 + nk - 1),
        out_specs=in_vmem(5),
        compiler_params=limits,
        name="final",
    )(kept, dq_in, dkv_own, *dkv_in)
    return tuple(
        out.reshape(slot_count, block_len, heads_here, out.shape[1]) for out in outs
    )


def solution(mesh):
    rows_spec = P("blk", None, "ulysses", None)
    in_specs = (rows_spec,) * 7 + (
        P("ulysses", None, "blk", None),
        P("ulysses"),
        P("ulysses", None),
        P("blk", "ulysses", None, None),
        P(),
    )
    shards = mesh.shape["blk"]
    body = functools.partial(one_device, shards, mesh.shape["ulysses"])
    return jax.shard_map(
        body, mesh=mesh, in_specs=in_specs, out_specs=(rows_spec,) * 5, check_vma=False
    )
```

```python
import functools
import math

import jax
import jax.numpy as jnp
from jax import lax
from jax.experimental import pallas as pl
from jax.experimental.pallas import tpu as pltpu
from jax.sharding import PartitionSpec as P


norm_eps = 1e-05
log2_e = math.log2(math.e)
VMEM = pltpu.VMEM
SMEM = pltpu.SMEM
f32 = jnp.float32
bf16 = jnp.bfloat16


def span(bits):
    masks = [0]
    for bit in bits:
        masks = masks + [mask ^ bit for mask in masks]
    return masks


def group_bits(shards):
    width = shards.bit_length() - 1
    bits = [1 << place for place in range(width)]
    middle = bits[1:-1]
    take = (width + 1) // 2
    key_bits = middle[:take]
    query_bits = [bit for bit in bits[::-1] if bit not in key_bits]
    return query_bits, key_bits


def send(member, mask, shards):
    return lax.ppermute(member, "blk", [(place, place ^ mask) for place in range(shards)])


def in_vmem(count):
    return [pl.BlockSpec(memory_space=VMEM)] * count


def in_smem(count):
    return [pl.BlockSpec(memory_space=SMEM)] * count


def three_parts(exact):
    high = exact.astype(bf16)
    rest = exact - high.astype(f32)
    middle = rest.astype(bf16)
    low = (rest - middle.astype(f32)).astype(bf16)
    return high, middle, low


def prepare_kernel(block_len, q_masks, k_masks, me, *refs):
    sources, (key_pack, query_pack, small, q_pos, k_pos) = refs[:8], refs[8:13]
    table, gain, logs, sems = refs[13:]
    rows, kw = sources[0].shape
    targets = [
        key_pack.at[:, :kw],
        key_pack.at[:, kw : 2 * kw],
        key_pack.at[:, 2 * kw :],
        query_pack.at[:, :kw],
        query_pack.at[:, kw:],
        gain,
        logs,
        table,
    ]
    copies = [
        pltpu.make_async_copy(source, target, sems.at[i])
        for i, (source, target) in enumerate(zip(sources, targets))
    ]
    for copy in copies[::-1]:
        copy.start()
    copies[7].wait()

    def places(mask, axis):
        shard = jnp.bitwise_xor(me[0], mask)
        low = table[2 * shard] * block_len
        high = (table[2 * shard + 1] - 1) * block_len
        shape = (rows, 1) if axis == 0 else (1, rows)
        offset = lax.broadcasted_iota(jnp.int32, shape, axis)
        return offset + jnp.where(offset < block_len, low, high)

    q_pos[...] = jnp.concatenate([places(mask, 1) for mask in q_masks], axis=1)
    for j, mask in enumerate(k_masks):
        k_pos[j * rows : (j + 1) * rows, :] = places(mask, 0)
    for copy in copies[:7]:
        copy.wait()
    width = gain.shape[1]
    wide_logs = jnp.concatenate(
        [logs[side, slot : slot + 1, :] for side in range(2) for slot in range(logs.shape[1])], axis=1
    )
    filler = jnp.zeros((small.shape[0] - 2, width), f32)
    small[...] = jnp.concatenate([gain[...], wide_logs, filler], axis=0)


def grad_out_kernel(place, lam, small, own_ref, other_ref, one_ref, two_ref, pack_ref):
    rows, width = one_ref.shape
    first = place[0] == 0
    own = jnp.where(first, own_ref[:, :, 0, :].astype(f32), own_ref[:, :, 1, :].astype(f32))
    other = jnp.where(first, other_ref[:, :, 0, :].astype(f32), other_ref[:, :, 1, :].astype(f32))
    upper = jnp.where(first, own, other)
    lower = jnp.where(first, other, own)
    grad_y = jnp.concatenate([upper, lower], axis=1).reshape(rows, width)
    one = one_ref[...].astype(f32)
    two = two_ref[...].astype(f32)
    combined = one - lam[0] * two
    inv_rms = lax.rsqrt(jnp.mean(combined * combined, axis=1, keepdims=True) + norm_eps)
    gained = small[0:1, :] * grad_y
    centre = jnp.mean(combined * gained, axis=1, keepdims=True)
    grad_out = (inv_rms * (gained - combined * inv_rms * inv_rms * centre)).astype(bf16)
    pack_ref[:rows, :] = grad_out
    wide = grad_out.astype(f32)

    def as_row(column):
        return jnp.transpose(jnp.broadcast_to(column, (rows, rows)))[:1, :]

    dot_one = as_row(jnp.sum(wide * one, axis=1, keepdims=True))
    dot_two = as_row(jnp.sum(wide * two, axis=1, keepdims=True))
    wide_dots = jnp.concatenate([dot_one, dot_two], axis=1)
    parts = three_parts(small[1:2, :]) + three_parts(wide_dots)
    filler = jnp.zeros((pack_ref.shape[0] - rows - len(parts), width), f32)
    pack_ref[rows:, :] = jnp.concatenate([part.astype(f32) for part in parts] + [filler], axis=0).astype(
        bf16
    )


def query_side(scale, lam, q_refs, do_refs, q_pos):
    rows, kw = q_refs[0].shape[0], q_refs[0].shape[1] // 2

    def stat(row, side):
        pieces = []
        for ref in do_refs:
            block = ref[rows:, side * rows : (side + 1) * rows].astype(f32)
            pieces.append(block[row : row + 1] + block[row + 1 : row + 2] + block[row + 2 : row + 3])
        return jnp.concatenate(pieces, axis=1)

    log_one = stat(0, 0) * -log2_e
    log_two = stat(0, 1) * -log2_e
    return (
        jnp.concatenate([ref[:, :kw] for ref in q_refs], axis=0),
        jnp.concatenate([ref[:, kw:] for ref in q_refs], axis=0),
        jnp.concatenate([ref[:rows, :] for ref in do_refs], axis=0),
        scale * log2_e,
        log_one,
        log_two + jnp.log(jnp.full(log_two.shape, lam, f32)) * log2_e,
        stat(3, 0),
        stat(3, 1),
        q_pos,
    )


def tile_terms(queries, k_refs, k_poss, own=False):
    q_one, q_two, grad, factor, log_one, log_two, dot_one, dot_two, q_pos = queries
    kw = q_one.shape[1]
    rows = k_refs[0].shape[0]
    contract = (((1,), (1,)), ((), ()))
    along_keys = (((0,), (0,)), ((), ()))
    k_one = jnp.concatenate([ref[:, :kw] for ref in k_refs], axis=0)
    k_two = jnp.concatenate([ref[:, kw : 2 * kw] for ref in k_refs], axis=0)
    val = jnp.concatenate([ref[:, 2 * kw :] for ref in k_refs], axis=0)
    s_one = lax.dot_general(k_one, q_one, contract, preferred_element_type=f32)
    s_two = lax.dot_general(k_two, q_two, contract, preferred_element_type=f32)
    d_attn = lax.dot_general(val, grad, contract, preferred_element_type=f32)

    def weights(score, log):
        score = score * factor
        parts = []
        for i, k_pos in enumerate(k_poss):
            if own and i == 0:
                seen = jnp.where(k_pos <= q_pos, score[:rows] + log, -jnp.inf)
                parts.append(jnp.exp2(seen))
                continue
            for first in (0, rows // 2):
                block = score[i * rows + first : i * rows + first + rows // 2]
                shift = jnp.where(k_pos[first : first + 1, :] <= q_pos, log, -jnp.inf)
                parts.append(jnp.exp2(block + shift))
        return jnp.concatenate(parts, axis=0)

    p_one = weights(s_one, log_one)
    p_two = weights(s_two, log_two)
    g_one = (p_one * (d_attn - dot_one)).astype(bf16)
    g_two = (p_two * (dot_two - d_attn)).astype(bf16)
    mix = (p_one - p_two).astype(bf16)
    return (
        jnp.dot(g_one, q_one, preferred_element_type=f32),
        jnp.dot(g_two, q_two, preferred_element_type=f32),
        jnp.dot(mix, grad, preferred_element_type=f32),
        lax.dot_general(g_one, k_one, along_keys, preferred_element_type=f32),
        lax.dot_general(g_two, k_two, along_keys, preferred_element_type=f32),
    )


def put_key_terms(outs, terms, befores=None):
    kw = terms[0].shape[1]
    for part, stacked in zip((slice(0, kw), slice(kw, 2 * kw), slice(2 * kw, None)), terms):
        for i, out in enumerate(outs):
            term = stacked[i * out.shape[0] : (i + 1) * out.shape[0]]
            out[:, part] = (term if befores is None else term + befores[i][:, part]).astype(out.dtype)


def key_rows(k_pos, place, rows):
    return k_pos[place * rows : (place + 1) * rows, :]


def tile_early_kernel(scale, half, places, lam, q_pos, k_pos, *refs):
    q_refs, do_refs, refs = refs[:half], refs[half : 2 * half], refs[2 * half :]
    k_refs, (dq_sum, *dkv) = refs[: len(places)], refs[len(places) :]
    rows = q_refs[0].shape[0]
    queries = query_side(scale, lam[0], q_refs, do_refs, q_pos[:, : half * rows])
    terms = tile_terms(queries, k_refs, [key_rows(k_pos, place, rows) for place in places], True)
    put_key_terms(dkv, terms[:3])
    kw = terms[3].shape[1]
    dq_sum[:, :kw], dq_sum[:, kw:] = terms[3:]


def tile_late_kernel(scale, half, places, whole_places, keep, sent, lam, q_pos, k_pos, *refs):
    count = len(places)
    q_refs, do_refs, refs = refs[: 2 * half], refs[2 * half : 4 * half], refs[4 * half :]
    k_refs, refs = refs[:count], refs[count:]
    whole_refs, refs = refs[: len(whole_places)], refs[len(whole_places) :]
    before, (dq_before, dq_keep, dq_send, *dkv) = refs[:count], refs[count:]
    rows, kw = q_refs[0].shape[0], q_refs[0].shape[1] // 2
    edge = half * rows
    late = query_side(scale, lam[0], q_refs[half:], do_refs[half:], q_pos[:, edge:])
    terms = tile_terms(late, k_refs, [key_rows(k_pos, place, rows) for place in places])
    put_key_terms(dkv[:count], terms[:3], before)
    late_sums = terms[3:]
    whole = query_side(scale, lam[0], q_refs, do_refs, q_pos[...])
    terms = tile_terms(whole, whole_refs, [key_rows(k_pos, place, rows) for place in whole_places])
    put_key_terms(dkv[count:], terms[:3])
    for out, order in ((dq_keep, keep), (dq_send, sent)):
        for slot, i in enumerate(order):
            here = slice(slot * rows, (slot + 1) * rows)
            for n, side in enumerate((slice(0, kw), slice(kw, None))):
                total = terms[3 + n][i * rows : (i + 1) * rows]
                if i < half:
                    total = total + dq_before[i * rows : (i + 1) * rows, side]
                else:
                    total = total + late_sums[n][i * rows - edge : (i + 1) * rows - edge]
                out[here, side] = total.astype(out.dtype)


def final_kernel(scale, count, dq_ref, dq_in, own_ref, *refs):
    dkv_in, outs = refs[:count], refs[count:]
    kw = outs[0].shape[1]
    dq = (dq_ref[...] + dq_in[...].astype(f32)) * scale
    outs[0][...] = dq[:, :kw].astype(bf16)
    outs[1][...] = dq[:, kw:].astype(bf16)
    total = own_ref[...]
    for ref in dkv_in:
        total = total + ref[...].astype(f32)
    outs[2][...] = (total[:, :kw] * scale).astype(bf16)
    outs[3][...] = (total[:, kw : 2 * kw] * scale).astype(bf16)
    outs[4][...] = total[:, 2 * kw :].astype(bf16)


def one_device(
    shards,
    ranks,
    query_first,
    query_second,
    key_first,
    key_second,
    values,
    out_first,
    out_second,
    log_totals,
    lambdas,
    norm_gain,
    cotangent,
    block_of,
):
    slot_count, block_len, heads_here, value_width = values.shape
    key_width = query_first.shape[3]
    rows = slot_count * block_len
    scale = 1.0 / math.sqrt(key_width)
    assert heads_here == 1 and slot_count == 2 and shards == 1 << (shards.bit_length() - 1)
    q_bits, k_bits = group_bits(shards)
    top = q_bits[-1]
    early_masks = [mask for mask in span(q_bits) if not mask & q_bits[0]]
    q_masks = early_masks + [mask ^ q_bits[0] for mask in early_masks]
    k_masks = span(k_bits)
    nq, nk = len(q_masks), len(k_masks)
    width = 2 * key_width + value_width
    me = lax.axis_index("blk").reshape(1).astype(jnp.int32)
    rank = lax.axis_index("ulysses").reshape(1).astype(jnp.int32)
    limits = pltpu.CompilerParams(vmem_limit_bytes=16 << 20)

    def flat(member):
        return member.reshape(rows, member.shape[3])

    if ranks == 2:
        own_half = cotangent
        other_half = lax.ppermute(cotangent, "ulysses", [(0, 1), (1, 0)])
    else:
        whole = lax.all_to_all(cotangent, "ulysses", split_axis=2, concat_axis=1, tiled=True)
        whole = jnp.concatenate([whole, whole], axis=2)
        own_half, other_half = whole[:, : block_len // 2], whole[:, block_len // 2 :]
        rank = jnp.zeros((1,), jnp.int32)

    key_pack, query_pack, small, q_pos, k_pos = pl.pallas_call(
        functools.partial(prepare_kernel, block_len, q_masks, k_masks),
        out_shape=[
            jax.ShapeDtypeStruct((rows, width), bf16),
            jax.ShapeDtypeStruct((rows, 2 * key_width), bf16),
            jax.ShapeDtypeStruct((8, value_width), f32),
            jax.ShapeDtypeStruct((1, nq * rows), jnp.int32),
            jax.ShapeDtypeStruct((nk * rows, 1), jnp.int32),
        ],
        in_specs=in_smem(1) + [pl.BlockSpec(memory_space=pltpu.HBM)] * 8,
        out_specs=in_vmem(5),
        scratch_shapes=[
            SMEM(block_of.shape, jnp.int32),
            VMEM((1, value_width), f32),
            VMEM((2, slot_count, block_len), f32),
            pltpu.SemaphoreType.DMA((8,)),
        ],
        compiler_params=limits,
        name="prepare",
    )(
        me,
        *[
            pltpu.with_memory_space_constraint(member, pltpu.HBM)
            for member in (
                flat(key_first),
                flat(key_second),
                flat(values),
                flat(query_first),
                flat(query_second),
                norm_gain,
                log_totals.reshape(2, slot_count, block_len),
                block_of,
            )
        ],
    )

    def spread(member, bits):
        held = {0: member}
        for bit in bits:
            for mask in list(held):
                held[mask ^ bit] = send(held[mask], bit, shards)
        return held

    keys = spread(key_pack, k_bits[::-1])
    queries = spread(query_pack, q_bits[:-1])
    held_masks = list(queries)
    both = send(jnp.concatenate([queries[mask] for mask in held_masks]), top, shards)
    for i, mask in enumerate(held_masks):
        queries[mask ^ top] = both[i * rows : (i + 1) * rows]
    grad_pack = pl.pallas_call(
        grad_out_kernel,
        out_shape=jax.ShapeDtypeStruct((rows + 8, value_width), bf16),
        in_specs=in_smem(2) + in_vmem(5),
        out_specs=pl.BlockSpec(memory_space=VMEM),
        compiler_params=limits,
        name="grad_out",
    )(rank, lambdas, small, own_half, other_half, flat(out_first), flat(out_second))
    grads = spread(grad_pack, q_bits)

    half = nq // 2
    keep_masks = [mask for mask in span(q_bits) if not mask & top]
    keep = [q_masks.index(mask) for mask in keep_masks]
    sent = [q_masks.index(mask ^ top) for mask in keep_masks]

    def query_parts(masks):
        return [queries[mask] for mask in masks] + [grads[mask] for mask in masks]

    def shape(row_count, columns, dtype):
        return jax.ShapeDtypeStruct((row_count, columns), dtype)

    def tile(kernel, outs, *operands):
        return pl.pallas_call(
            kernel,
            out_shape=outs,
            in_specs=in_smem(1) + in_vmem(2 + len(operands)),
            out_specs=in_vmem(len(outs)),
            compiler_params=limits,
        )(lambdas, q_pos, k_pos, *operands)

    early = [0] + [k_masks.index(k_bits[-1])]
    whole = [j for j in range(nk) if j not in early]
    far = early[1:] + whole
    dq_early, *early_parts = tile(
        functools.partial(tile_early_kernel, scale, half, early),
        [shape(half * rows, 2 * key_width, f32)] + [shape(rows, width, f32)] * len(early),
        *query_parts(q_masks[:half]),
        *[keys[k_masks[j]] for j in early],
    )
    dq_keep, dq_send, dkv_own, *far_parts = tile(
        functools.partial(tile_late_kernel, scale, half, early, whole, keep, sent),
        [
            shape(half * rows, 2 * key_width, f32),
            shape(half * rows, 2 * key_width, bf16),
            shape(rows, width, f32),
        ]
        + [shape(rows, width, bf16)] * (nk - 1),
        *query_parts(q_masks),
        *[keys[k_masks[j]] for j in early + whole],
        *early_parts,
        dq_early,
    )
    held = dict(zip(far, far_parts))
    dkv_in = [send(held[j], k_masks[j], shards) for j in range(1, nk)]
    arrived = send(dq_send, top, shards)
    kept = dq_keep + arrived.astype(f32)
    for bit in q_bits[-2::-1]:
        size = kept.shape[0] // 2
        dq_in = send(kept[size:].astype(bf16), bit, shards)
        kept = kept[:size]
        if bit != q_bits[0]:
            kept = kept + dq_in.astype(f32)
    outs = pl.pallas_call(
        functools.partial(final_kernel, scale, nk - 1),
        out_shape=[jax.ShapeDtypeStruct((rows, key_width), bf16)] * 4
        + [jax.ShapeDtypeStruct((rows, value_width), bf16)],
        in_specs=in_vmem(3 + nk - 1),
        out_specs=in_vmem(5),
        compiler_params=limits,
        name="final",
    )(kept, dq_in, dkv_own, *dkv_in)
    return tuple(
        out.reshape(slot_count, block_len, heads_here, out.shape[1]) for out in outs
    )


def solution(mesh):
    rows_spec = P("blk", None, "ulysses", None)
    in_specs = (rows_spec,) * 7 + (
        P("ulysses", None, "blk", None),
        P("ulysses"),
        P("ulysses", None),
        P("blk", "ulysses", None, None),
        P(),
    )
    shards = mesh.shape["blk"]
    body = functools.partial(one_device, shards, mesh.shape["ulysses"])
    return jax.shard_map(
        body, mesh=mesh, in_specs=in_specs, out_specs=(rows_spec,) * 5, check_vma=False
    )
```

```python
import functools
import math

import jax
import jax.numpy as jnp
from jax import lax
from jax.experimental import pallas as pl
from jax.experimental.pallas import tpu as pltpu
from jax.sharding import PartitionSpec as P


norm_eps = 1e-05
log2_e = math.log2(math.e)
VMEM = pltpu.VMEM
SMEM = pltpu.SMEM
f32 = jnp.float32
bf16 = jnp.bfloat16


def span(bits):
    masks = [0]
    for bit in bits:
        masks = masks + [mask ^ bit for mask in masks]
    return masks


def group_bits(shards):
    width = shards.bit_length() - 1
    bits = [1 << place for place in range(width)]
    middle = bits[1:-1]
    take = (width + 1) // 2
    key_bits = middle[:take]
    query_bits = [bit for bit in bits[::-1] if bit not in key_bits]
    return query_bits, key_bits


def send(member, mask, shards):
    return lax.ppermute(member, "blk", [(place, place ^ mask) for place in range(shards)])


def in_vmem(count):
    return [pl.BlockSpec(memory_space=VMEM)] * count


def in_smem(count):
    return [pl.BlockSpec(memory_space=SMEM)] * count


def three_parts(exact):
    high = exact.astype(bf16)
    rest = exact - high.astype(f32)
    middle = rest.astype(bf16)
    low = (rest - middle.astype(f32)).astype(bf16)
    return high, middle, low


def prepare_kernel(block_len, q_masks, k_masks, me, *refs):
    sources, (key_pack, query_pack, small, q_pos, k_pos) = refs[:8], refs[8:13]
    table, gain, logs, sems = refs[13:]
    rows, kw = sources[0].shape
    targets = [
        key_pack.at[:, :kw],
        key_pack.at[:, kw : 2 * kw],
        key_pack.at[:, 2 * kw :],
        query_pack.at[:, :kw],
        query_pack.at[:, kw:],
        gain,
        logs,
        table,
    ]
    copies = [
        pltpu.make_async_copy(source, target, sems.at[i])
        for i, (source, target) in enumerate(zip(sources, targets))
    ]
    for copy in copies[::-1]:
        copy.start()
    copies[7].wait()

    def places(mask, axis):
        shard = jnp.bitwise_xor(me[0], mask)
        low = table[2 * shard] * block_len
        high = (table[2 * shard + 1] - 1) * block_len
        shape = (rows, 1) if axis == 0 else (1, rows)
        offset = lax.broadcasted_iota(jnp.int32, shape, axis)
        return offset + jnp.where(offset < block_len, low, high)

    q_pos[...] = jnp.concatenate([places(mask, 1) for mask in q_masks], axis=1)
    for j, mask in enumerate(k_masks):
        k_pos[j * rows : (j + 1) * rows, :] = places(mask, 0)
    for copy in copies[:7]:
        copy.wait()
    width = gain.shape[1]
    wide_logs = jnp.concatenate(
        [logs[side, slot : slot + 1, :] for side in range(2) for slot in range(logs.shape[1])], axis=1
    )
    filler = jnp.zeros((small.shape[0] - 2, width), f32)
    small[...] = jnp.concatenate([gain[...], wide_logs, filler], axis=0)


def grad_out_kernel(place, lam, small, own_ref, other_ref, one_ref, two_ref, pack_ref):
    rows, width = one_ref.shape
    first = place[0] == 0
    own = jnp.where(first, own_ref[:, :, 0, :].astype(f32), own_ref[:, :, 1, :].astype(f32))
    other = jnp.where(first, other_ref[:, :, 0, :].astype(f32), other_ref[:, :, 1, :].astype(f32))
    upper = jnp.where(first, own, other)
    lower = jnp.where(first, other, own)
    grad_y = jnp.concatenate([upper, lower], axis=1).reshape(rows, width)
    one = one_ref[...].astype(f32)
    two = two_ref[...].astype(f32)
    combined = one - lam[0] * two
    inv_rms = lax.rsqrt(jnp.mean(combined * combined, axis=1, keepdims=True) + norm_eps)
    gained = small[0:1, :] * grad_y
    centre = jnp.mean(combined * gained, axis=1, keepdims=True)
    grad_out = (inv_rms * (gained - combined * inv_rms * inv_rms * centre)).astype(bf16)
    pack_ref[:rows, :] = grad_out
    wide = grad_out.astype(f32)

    def as_row(column):
        return jnp.transpose(jnp.broadcast_to(column, (rows, rows)))[:1, :]

    dot_one = as_row(jnp.sum(wide * one, axis=1, keepdims=True))
    dot_two = as_row(jnp.sum(wide * two, axis=1, keepdims=True))
    wide_dots = jnp.concatenate([dot_one, dot_two], axis=1)
    parts = three_parts(small[1:2, :]) + three_parts(wide_dots)
    filler = jnp.zeros((pack_ref.shape[0] - rows - len(parts), width), f32)
    pack_ref[rows:, :] = jnp.concatenate([part.astype(f32) for part in parts] + [filler], axis=0).astype(
        bf16
    )


def query_side(scale, lam, q_refs, do_refs, q_pos):
    rows, kw = q_refs[0].shape[0], q_refs[0].shape[1] // 2

    def stat(row, side):
        pieces = []
        for ref in do_refs:
            block = ref[rows:, side * rows : (side + 1) * rows].astype(f32)
            pieces.append(block[row : row + 1] + block[row + 1 : row + 2] + block[row + 2 : row + 3])
        return jnp.concatenate(pieces, axis=1)

    log_one = stat(0, 0) * -log2_e
    log_two = stat(0, 1) * -log2_e
    return (
        jnp.concatenate([ref[:, :kw] for ref in q_refs], axis=0),
        jnp.concatenate([ref[:, kw:] for ref in q_refs], axis=0),
        jnp.concatenate([ref[:rows, :] for ref in do_refs], axis=0),
        scale * log2_e,
        log_one,
        log_two + jnp.log(jnp.full(log_two.shape, lam, f32)) * log2_e,
        stat(3, 0),
        stat(3, 1),
        q_pos,
    )


def tile_terms(queries, k_refs, k_poss, own=False):
    q_one, q_two, grad, factor, log_one, log_two, dot_one, dot_two, q_pos = queries
    kw = q_one.shape[1]
    rows = k_refs[0].shape[0]
    contract = (((1,), (1,)), ((), ()))
    along_keys = (((0,), (0,)), ((), ()))
    k_one = jnp.concatenate([ref[:, :kw] for ref in k_refs], axis=0)
    k_two = jnp.concatenate([ref[:, kw : 2 * kw] for ref in k_refs], axis=0)
    val = jnp.concatenate([ref[:, 2 * kw :] for ref in k_refs], axis=0)
    s_one = lax.dot_general(k_one, q_one, contract, preferred_element_type=f32)
    s_two = lax.dot_general(k_two, q_two, contract, preferred_element_type=f32)
    d_attn = lax.dot_general(val, grad, contract, preferred_element_type=f32)

    def weights(score, log):
        score = score * factor
        parts = []
        for i, k_pos in enumerate(k_poss):
            if own and i == 0:
                seen = jnp.where(k_pos <= q_pos, score[:rows] + log, -jnp.inf)
                parts.append(jnp.exp2(seen))
                continue
            for first in (0, rows // 2):
                block = score[i * rows + first : i * rows + first + rows // 2]
                shift = jnp.where(k_pos[first : first + 1, :] <= q_pos, log, -jnp.inf)
                parts.append(jnp.exp2(block + shift))
        return jnp.concatenate(parts, axis=0)

    p_one = weights(s_one, log_one)
    p_two = weights(s_two, log_two)
    g_one = (p_one * (d_attn - dot_one)).astype(bf16)
    g_two = (p_two * (dot_two - d_attn)).astype(bf16)
    mix = (p_one - p_two).astype(bf16)
    return (
        jnp.dot(g_one, q_one, preferred_element_type=f32),
        jnp.dot(g_two, q_two, preferred_element_type=f32),
        jnp.dot(mix, grad, preferred_element_type=f32),
        lax.dot_general(g_one, k_one, along_keys, preferred_element_type=f32),
        lax.dot_general(g_two, k_two, along_keys, preferred_element_type=f32),
    )


def put_key_terms(outs, terms, befores=None):
    kw = terms[0].shape[1]
    for part, stacked in zip((slice(0, kw), slice(kw, 2 * kw), slice(2 * kw, None)), terms):
        for i, out in enumerate(outs):
            term = stacked[i * out.shape[0] : (i + 1) * out.shape[0]]
            out[:, part] = (term if befores is None else term + befores[i][:, part]).astype(out.dtype)


def key_rows(k_pos, place, rows):
    return k_pos[place * rows : (place + 1) * rows, :]


def tile_early_kernel(scale, half, places, lam, q_pos, k_pos, *refs):
    q_refs, do_refs, refs = refs[:half], refs[half : 2 * half], refs[2 * half :]
    k_refs, (dq_sum, *dkv) = refs[: len(places)], refs[len(places) :]
    rows = q_refs[0].shape[0]
    queries = query_side(scale, lam[0], q_refs, do_refs, q_pos[:, : half * rows])
    terms = tile_terms(queries, k_refs, [key_rows(k_pos, place, rows) for place in places], True)
    put_key_terms(dkv, terms[:3])
    kw = terms[3].shape[1]
    dq_sum[:, :kw], dq_sum[:, kw:] = terms[3:]


def tile_late_kernel(scale, half, places, whole_places, keep, sent, lam, q_pos, k_pos, *refs):
    count = len(places)
    q_refs, do_refs, refs = refs[: 2 * half], refs[2 * half : 4 * half], refs[4 * half :]
    k_refs, refs = refs[:count], refs[count:]
    whole_refs, refs = refs[: len(whole_places)], refs[len(whole_places) :]
    before, (dq_before, dq_keep, dq_send, *dkv) = refs[:count], refs[count:]
    rows, kw = q_refs[0].shape[0], q_refs[0].shape[1] // 2
    edge = half * rows
    late = query_side(scale, lam[0], q_refs[half:], do_refs[half:], q_pos[:, edge:])
    near = query_side(scale, lam[0], q_refs[:half], do_refs[:half], q_pos[:, :edge])
    near_terms = tile_terms(near, whole_refs, [key_rows(k_pos, place, rows) for place in whole_places])
    every = list(places) + list(whole_places)
    terms = tile_terms(
        late, list(k_refs) + list(whole_refs), [key_rows(k_pos, place, rows) for place in every]
    )
    put_key_terms(dkv[:count], [term[: count * rows] for term in terms[:3]], before)
    put_key_terms(
        dkv[count:], [term[count * rows :] + old for term, old in zip(terms[:3], near_terms[:3])]
    )
    late_sums, near_sums = terms[3:], near_terms[3:]
    for out, order in ((dq_keep, keep), (dq_send, sent)):
        for slot, i in enumerate(order):
            here = slice(slot * rows, (slot + 1) * rows)
            for n, side in enumerate((slice(0, kw), slice(kw, None))):
                if i < half:
                    mine = slice(i * rows, (i + 1) * rows)
                    total = near_sums[n][mine] + dq_before[mine, side]
                else:
                    total = late_sums[n][i * rows - edge : (i + 1) * rows - edge]
                out[here, side] = total.astype(out.dtype)


def final_kernel(scale, count, dq_ref, dq_in, own_ref, *refs):
    dkv_in, outs = refs[:count], refs[count:]
    kw = outs[0].shape[1]
    dq = (dq_ref[...] + dq_in[...].astype(f32)) * scale
    outs[0][...] = dq[:, :kw].astype(bf16)
    outs[1][...] = dq[:, kw:].astype(bf16)
    total = own_ref[...]
    for ref in dkv_in:
        total = total + ref[...].astype(f32)
    outs[2][...] = (total[:, :kw] * scale).astype(bf16)
    outs[3][...] = (total[:, kw : 2 * kw] * scale).astype(bf16)
    outs[4][...] = total[:, 2 * kw :].astype(bf16)


def one_device(
    shards,
    ranks,
    query_first,
    query_second,
    key_first,
    key_second,
    values,
    out_first,
    out_second,
    log_totals,
    lambdas,
    norm_gain,
    cotangent,
    block_of,
):
    slot_count, block_len, heads_here, value_width = values.shape
    key_width = query_first.shape[3]
    rows = slot_count * block_len
    scale = 1.0 / math.sqrt(key_width)
    assert heads_here == 1 and slot_count == 2 and shards == 1 << (shards.bit_length() - 1)
    q_bits, k_bits = group_bits(shards)
    top = q_bits[-1]
    early_masks = [mask for mask in span(q_bits) if not mask & q_bits[0]]
    q_masks = early_masks + [mask ^ q_bits[0] for mask in early_masks]
    k_masks = span(k_bits)
    nq, nk = len(q_masks), len(k_masks)
    width = 2 * key_width + value_width
    me = lax.axis_index("blk").reshape(1).astype(jnp.int32)
    rank = lax.axis_index("ulysses").reshape(1).astype(jnp.int32)
    limits = pltpu.CompilerParams(vmem_limit_bytes=16 << 20)

    def flat(member):
        return member.reshape(rows, member.shape[3])

    if ranks == 2:
        own_half = cotangent
        other_half = lax.ppermute(cotangent, "ulysses", [(0, 1), (1, 0)])
    else:
        whole = lax.all_to_all(cotangent, "ulysses", split_axis=2, concat_axis=1, tiled=True)
        whole = jnp.concatenate([whole, whole], axis=2)
        own_half, other_half = whole[:, : block_len // 2], whole[:, block_len // 2 :]
        rank = jnp.zeros((1,), jnp.int32)

    key_pack, query_pack, small, q_pos, k_pos = pl.pallas_call(
        functools.partial(prepare_kernel, block_len, q_masks, k_masks),
        out_shape=[
            jax.ShapeDtypeStruct((rows, width), bf16),
            jax.ShapeDtypeStruct((rows, 2 * key_width), bf16),
            jax.ShapeDtypeStruct((8, value_width), f32),
            jax.ShapeDtypeStruct((1, nq * rows), jnp.int32),
            jax.ShapeDtypeStruct((nk * rows, 1), jnp.int32),
        ],
        in_specs=in_smem(1) + [pl.BlockSpec(memory_space=pltpu.HBM)] * 8,
        out_specs=in_vmem(5),
        scratch_shapes=[
            SMEM(block_of.shape, jnp.int32),
            VMEM((1, value_width), f32),
            VMEM((2, slot_count, block_len), f32),
            pltpu.SemaphoreType.DMA((8,)),
        ],
        compiler_params=limits,
        name="prepare",
    )(
        me,
        *[
            pltpu.with_memory_space_constraint(member, pltpu.HBM)
            for member in (
                flat(key_first),
                flat(key_second),
                flat(values),
                flat(query_first),
                flat(query_second),
                norm_gain,
                log_totals.reshape(2, slot_count, block_len),
                block_of,
            )
        ],
    )

    def spread(member, bits):
        held = {0: member}
        for bit in bits:
            for mask in list(held):
                held[mask ^ bit] = send(held[mask], bit, shards)
        return held

    keys = spread(key_pack, k_bits[::-1])
    queries = spread(query_pack, q_bits[:-1])
    held_masks = list(queries)
    both = send(jnp.concatenate([queries[mask] for mask in held_masks]), top, shards)
    for i, mask in enumerate(held_masks):
        queries[mask ^ top] = both[i * rows : (i + 1) * rows]
    grad_pack = pl.pallas_call(
        grad_out_kernel,
        out_shape=jax.ShapeDtypeStruct((rows + 8, value_width), bf16),
        in_specs=in_smem(2) + in_vmem(5),
        out_specs=pl.BlockSpec(memory_space=VMEM),
        compiler_params=limits,
        name="grad_out",
    )(rank, lambdas, small, own_half, other_half, flat(out_first), flat(out_second))
    grads = spread(grad_pack, q_bits)

    half = nq // 2
    keep_masks = [mask for mask in span(q_bits) if not mask & top]
    keep = [q_masks.index(mask) for mask in keep_masks]
    sent = [q_masks.index(mask ^ top) for mask in keep_masks]

    def query_parts(masks):
        return [queries[mask] for mask in masks] + [grads[mask] for mask in masks]

    def shape(row_count, columns, dtype):
        return jax.ShapeDtypeStruct((row_count, columns), dtype)

    def tile(kernel, outs, *operands):
        return pl.pallas_call(
            kernel,
            out_shape=outs,
            in_specs=in_smem(1) + in_vmem(2 + len(operands)),
            out_specs=in_vmem(len(outs)),
            compiler_params=limits,
        )(lambdas, q_pos, k_pos, *operands)

    early = [0] + [k_masks.index(k_bits[-1])]
    whole = [j for j in range(nk) if j not in early]
    far = early[1:] + whole
    dq_early, *early_parts = tile(
        functools.partial(tile_early_kernel, scale, half, early),
        [shape(half * rows, 2 * key_width, f32)] + [shape(rows, width, f32)] * len(early),
        *query_parts(q_masks[:half]),
        *[keys[k_masks[j]] for j in early],
    )
    dq_keep, dq_send, dkv_own, *far_parts = tile(
        functools.partial(tile_late_kernel, scale, half, early, whole, keep, sent),
        [
            shape(half * rows, 2 * key_width, f32),
            shape(half * rows, 2 * key_width, bf16),
            shape(rows, width, f32),
        ]
        + [shape(rows, width, bf16)] * (nk - 1),
        *query_parts(q_masks),
        *[keys[k_masks[j]] for j in early + whole],
        *early_parts,
        dq_early,
    )
    held = dict(zip(far, far_parts))
    dkv_in = [send(held[j], k_masks[j], shards) for j in range(1, nk)]
    arrived = send(dq_send, top, shards)
    kept = dq_keep + arrived.astype(f32)
    for bit in q_bits[-2::-1]:
        size = kept.shape[0] // 2
        dq_in = send(kept[size:].astype(bf16), bit, shards)
        kept = kept[:size]
        if bit != q_bits[0]:
            kept = kept + dq_in.astype(f32)
    outs = pl.pallas_call(
        functools.partial(final_kernel, scale, nk - 1),
        out_shape=[jax.ShapeDtypeStruct((rows, key_width), bf16)] * 4
        + [jax.ShapeDtypeStruct((rows, value_width), bf16)],
        in_specs=in_vmem(3 + nk - 1),
        out_specs=in_vmem(5),
        compiler_params=limits,
        name="final",
    )(kept, dq_in, dkv_own, *dkv_in)
    return tuple(
        out.reshape(slot_count, block_len, heads_here, out.shape[1]) for out in outs
    )


def solution(mesh):
    rows_spec = P("blk", None, "ulysses", None)
    in_specs = (rows_spec,) * 7 + (
        P("ulysses", None, "blk", None),
        P("ulysses"),
        P("ulysses", None),
        P("blk", "ulysses", None, None),
        P(),
    )
    shards = mesh.shape["blk"]
    body = functools.partial(one_device, shards, mesh.shape["ulysses"])
    return jax.shard_map(
        body, mesh=mesh, in_specs=in_specs, out_specs=(rows_spec,) * 5, check_vma=False
    )
```
